128 devices in a mesh: fsdp: 4 (over y), ctx: 16 (over z, x), tp: 2 (over core).
Axes of the slice: x: 4, y: 4, z: 4, core: 2. Of those that a mesh axis runs over, the one named last changes fastest.
Arguments:
- inputs: float32 [8, 2048, 896], P('fsdp', 'ctx'), may hold values from -6 to 6
- block_order: int32 [8, 32], P('fsdp'), may hold values from 0 to 31, as said below
- cotangent: float32 [8, 2048, 896], P('fsdp', 'ctx'), may hold values from -6 to 6
- gains: bfloat16 [1, 2, 896], P(None, None, ('fsdp', 'ctx')), may hold values from 0.5 to 1.5
- w_qkv: bfloat16 [1, 896, 2, 576], P(None, ('fsdp', 'ctx'), 'tp'), may hold values from -0.1875 to 0.1875
- b_qkv: bfloat16 [1, 2, 9, 64], P(None, 'tp', None, ('fsdp', 'ctx')), may hold values from -1 to 1
- w_out: bfloat16 [1, 2, 448, 896], P(None, 'tp', None, ('fsdp', 'ctx')), may hold values from -1.5 to 1.5
- w_gate_up: bfloat16 [1, 896, 2, 4864], P(None, ('fsdp', 'ctx'), None, 'tp'), may hold values from -0.1875 to 0.1875
- w_down: bfloat16 [1, 4864, 896], P(None, 'tp', ('fsdp', 'ctx')), may hold values from -0.078125 to 0.078125
Outputs:
- outputs: float32 [8, 2048, 896], P('fsdp', 'ctx')
- grad_inputs: float32 [8, 2048, 896], P('fsdp', 'ctx')
- grad_gains: float32 [1, 2, 896], P(None, None, ('fsdp', 'ctx'))
- grad_w_qkv: float32 [1, 896, 2, 576], P(None, ('fsdp', 'ctx'), 'tp')
- grad_b_qkv: float32 [1, 2, 9, 64], P(None, 'tp', None, ('fsdp', 'ctx'))
- grad_w_out: float32 [1, 2, 448, 896], P(None, 'tp', None, ('fsdp', 'ctx'))
- grad_w_gate_up: float32 [1, 896, 2, 4864], P(None, ('fsdp', 'ctx'), None, 'tp')
- grad_w_down: float32 [1, 4864, 896], P(None, 'tp', ('fsdp', 'ctx'))
The draws below stay inside these ranges and needn't reach their ends.
Inputs may be any that keep to these rules, and one draw needn't show every extreme that they name: `block_order`: each row holds every number 0 to 31 once, and entries 2 c and 2 c + 1 of a row add up to 31.
All inputs are finite; a program needn't handle non-finite values.
Results may differ from the reference program's by a relative error of at most 0.019.
Values may be sent and summed in bfloat16 or wider, within the bound.
No kernel may reach another device: no remote copies, remote signals or barrier semaphores. Data moves between devices by JAX's collectives and lax.ppermute only.
A program may use at most 192 MiB of HBM per device.

```python
import math
import jax
import jax.numpy as jnp
from jax import lax

D = 896
FF = 4864
HEADS = 14
KV_HEADS = 2
HEAD_DIM = 64
LAYERS = 1
BLOCK_LEN = 64
SEQS = 8
LEN = 2048
N_CTX = 16
N_TP = 2


def one_permutation(subkey):
    return jax.random.permutation(subkey, N_CTX)


def draw_block_order(key, part):
    subkeys = jax.random.split(key, SEQS)
    picks = jax.vmap(one_permutation)(subkeys).astype(jnp.int32)
    mirror = 2 * N_CTX - 1 - picks
    return jnp.stack([picks, mirror], axis=-1).reshape(SEQS, 2 * N_CTX).astype(jnp.int32)


def levels(own_key, extent, pieces, least, top_value):
    factor_of = 1.0
    for position, parts in pieces:
        steps = jax.random.uniform(jax.random.fold_in(jax.random.fold_in(own_key, 6), position), (parts,), jnp.float32, least / len(pieces), top_value / len(pieces))
        factor_of = factor_of * jnp.repeat(jnp.exp(steps), extent[position] // parts).reshape((-1,) + (1,) * (len(extent) - 1 - position))
    return factor_of


def normal_values(own_key, extent, scale, bound, shards=(), kind=jnp.bfloat16):
    factor_of = levels(own_key, extent, shards, -0.22, 0.18) if shards else 1.0
    entries = jax.random.normal(own_key, extent, jnp.float32) * scale * factor_of
    return jnp.minimum(jnp.maximum(entries, -bound), bound).astype(kind)


def setup_inputs(seed: int = 0) -> dict:
    splits = jax.random.split(jax.random.key(seed), 10)
    inputs = normal_values(splits[0], (SEQS, LEN, D), 1.0, 6.0, ((0, 4), (1, 16)), jnp.float32)
    block_order = draw_block_order(jax.random.fold_in(splits[9], 71), 0)
    cotangent = normal_values(splits[2], (SEQS, LEN, D), 1.0, 6.0, ((0, 4), (1, 16)), jnp.float32)
    gains = jnp.clip(1.0 + 0.1 * jax.random.normal(splits[3], (LAYERS, 2, D), jnp.float32), 0.5, 1.5).astype(jnp.bfloat16)
    w_qkv = normal_values(splits[4], (LAYERS, D, N_TP, (HEADS + 2 * KV_HEADS) * HEAD_DIM // N_TP), D ** -0.5, 0.1875, ((1, 64), (2, 2)))
    b_qkv = normal_values(splits[5], (LAYERS, N_TP, (HEADS + 2 * KV_HEADS) // N_TP, HEAD_DIM), 0.2, 1.0, ((1, 2), (3, 64)))
    w_out = normal_values(splits[6], (LAYERS, N_TP, HEADS * HEAD_DIM // N_TP, D), 16 ** -0.5, 1.5, ((1, 2), (3, 64)))
    w_gate_up = normal_values(splits[7], (LAYERS, D, 2, FF), D ** -0.5, 0.1875, ((1, 64), (3, 2)))
    w_down = normal_values(splits[8], (LAYERS, FF, D), FF ** -0.5, 0.078125, ((1, 2), (2, 64)))
    return {"inputs": inputs, "block_order": block_order, "cotangent": cotangent, "gains": gains, "w_qkv": w_qkv, "b_qkv": b_qkv, "w_out": w_out, "w_gate_up": w_gate_up, "w_down": w_down}


epsilon = 1e-06
rope_base = 1000000.0
masked_score = -1e+30

def rms_forward(hidden, gain_vector):
    scale_rows = lax.rsqrt(lax.optimization_barrier(jnp.mean(hidden * hidden, axis=-1, keepdims=True)) + epsilon)
    unit_rows = hidden * scale_rows
    return (unit_rows, scale_rows, (unit_rows * gain_vector.astype(jnp.float32)).astype(jnp.bfloat16))

def rms_backward(grad_normed, unit_rows, scale_rows, gain_vector):
    grad_gain = lax.optimization_barrier(jnp.sum(grad_normed * unit_rows, axis=0))
    grad_unit = grad_normed * gain_vector.astype(jnp.float32)
    grad_hidden = scale_rows * (grad_unit - unit_rows * lax.optimization_barrier(jnp.mean(grad_unit * unit_rows, axis=-1, keepdims=True)))
    return (grad_hidden, grad_gain)

def rotary(positions):
    half_dim = HEAD_DIM // 2
    freq_steps = jnp.arange(half_dim, dtype=jnp.float32)
    frequency = jnp.exp(freq_steps * (-2.0 * math.log(rope_base) / HEAD_DIM))
    angles = positions.astype(jnp.float32)[:, None] * frequency[None, :]
    return (jnp.cos(angles), jnp.sin(angles))

def rotate(vectors, cosine, sine_table):
    half_dim = vectors.shape[-1] // 2
    first_half = vectors[..., :half_dim]
    second_half = vectors[..., half_dim:]
    return jnp.concatenate([first_half * cosine - second_half * sine_table, second_half * cosine + first_half * sine_table], axis=-1)

def rotate_back(vectors, cosine, sine_table):
    half_dim = vectors.shape[-1] // 2
    first_half = vectors[..., :half_dim]
    second_half = vectors[..., half_dim:]
    return jnp.concatenate([first_half * cosine + second_half * sine_table, second_half * cosine - first_half * sine_table], axis=-1)

def split_columns(projected):
    length = projected.shape[0]
    blocks = projected.reshape(length, N_TP, -1)
    q_width = HEADS // N_TP * HEAD_DIM
    kv_width = KV_HEADS // N_TP * HEAD_DIM
    query_raw = blocks[:, :, :q_width].reshape(length, KV_HEADS, HEADS // KV_HEADS, HEAD_DIM)
    key_raw = blocks[:, :, q_width:q_width + kv_width].reshape(length, KV_HEADS, HEAD_DIM)
    value_raw = blocks[:, :, q_width + kv_width:].reshape(length, KV_HEADS, HEAD_DIM)
    return (query_raw, key_raw, value_raw)

def join_columns(d_query, d_key, d_value):
    length = d_query.shape[0]
    joined = jnp.concatenate([d_query.reshape(length, N_TP, -1), d_key.reshape(length, N_TP, -1), d_value.reshape(length, N_TP, -1)], axis=2)
    return joined.reshape(length, -1)

def scores_of(query_rows, key_rows, positions):
    raw_scores = jnp.einsum('qkgd,lkd->kgql', query_rows.astype(jnp.float32), key_rows.astype(jnp.float32))
    raw_scores = raw_scores * (1.0 / math.sqrt(HEAD_DIM))
    allowed = positions[None, None, None, :] <= positions[None, None, :, None]
    return jnp.where(allowed, raw_scores, masked_score)

def layer_forward(hidden, positions, cosine, sine_table, weights):
    qkv_w, qkv_b, out_w, gate_up_w, down_w, gain_pair = weights
    length = hidden.shape[0]
    first_unit, first_scale, first_normed = rms_forward(hidden, gain_pair[0])
    projected = jnp.dot(first_normed, qkv_w, preferred_element_type=jnp.float32) + qkv_b.astype(jnp.float32)
    query_raw, key_raw, value_raw = split_columns(projected)
    query_rows = rotate(query_raw, cosine[:, None, None, :], sine_table[:, None, None, :]).astype(jnp.bfloat16)
    key_rows = rotate(key_raw, cosine[:, None, :], sine_table[:, None, :]).astype(jnp.bfloat16)
    value_rows = value_raw.astype(jnp.bfloat16)
    scores = scores_of(query_rows, key_rows, positions)
    row_top = lax.optimization_barrier(jnp.max(scores, axis=-1, keepdims=True))
    log_total = row_top + jnp.log(lax.optimization_barrier(jnp.sum(jnp.exp(scores - row_top), axis=-1, keepdims=True)))
    probs_low = jnp.exp(scores - log_total).astype(jnp.bfloat16)
    attended = jnp.einsum('kgql,lkd->qkgd', probs_low.astype(jnp.float32), value_rows.astype(jnp.float32)).astype(jnp.bfloat16)
    mixed_rows = hidden + jnp.dot(attended.reshape(length, -1), out_w, preferred_element_type=jnp.float32)
    second_unit, second_scale, second_normed = rms_forward(mixed_rows, gain_pair[1])
    gate_part = jnp.dot(second_normed, gate_up_w[:, 0, :], preferred_element_type=jnp.float32)
    up_part = jnp.dot(second_normed, gate_up_w[:, 1, :], preferred_element_type=jnp.float32)
    activated = (jax.nn.silu(gate_part) * up_part).astype(jnp.bfloat16)
    result_rows = mixed_rows + jnp.dot(activated, down_w, preferred_element_type=jnp.float32)
    saved_state = (first_unit, first_scale, first_normed, query_rows, key_rows, value_rows, log_total, attended, second_unit, second_scale, second_normed, gate_part, up_part, activated)
    return (result_rows, saved_state)

def layer_backward(gradient, saved_state, positions, cosine, sine_table, weights):
    qkv_w, qkv_b, out_w, gate_up_w, down_w, gain_pair = weights
    first_unit, first_scale, first_normed, query_rows, key_rows, value_rows, log_total, attended, second_unit, second_scale, second_normed, gate_part, up_part, activated = saved_state
    length = gradient.shape[0]
    grad_low = gradient.astype(jnp.bfloat16)
    grad_down = jnp.dot(activated.T, grad_low, preferred_element_type=jnp.float32)
    d_activated = jnp.dot(grad_low, down_w.T, preferred_element_type=jnp.float32)
    sigmoid_gate = jax.nn.sigmoid(gate_part)
    d_gate = (d_activated * up_part * sigmoid_gate * (1.0 + gate_part * (1.0 - sigmoid_gate))).astype(jnp.bfloat16)
    d_up = (d_activated * (gate_part * sigmoid_gate)).astype(jnp.bfloat16)
    grad_gate_up = jnp.stack([jnp.dot(second_normed.T, d_gate, preferred_element_type=jnp.float32), jnp.dot(second_normed.T, d_up, preferred_element_type=jnp.float32)], axis=1)
    d_second = jnp.dot(d_gate, gate_up_w[:, 0, :].T, preferred_element_type=jnp.float32) + jnp.dot(d_up, gate_up_w[:, 1, :].T, preferred_element_type=jnp.float32)
    d_middle, grad_gain_two = rms_backward(d_second, second_unit, second_scale, gain_pair[1])
    d_mixed = gradient + d_middle
    d_mixed_low = d_mixed.astype(jnp.bfloat16)
    grad_out = jnp.dot(attended.reshape(length, -1).T, d_mixed_low, preferred_element_type=jnp.float32)
    d_attended = jnp.dot(d_mixed_low, out_w.T, preferred_element_type=jnp.float32).astype(jnp.bfloat16)
    d_attended = d_attended.reshape(attended.shape)
    scores = scores_of(query_rows, key_rows, positions)
    probs_full = jnp.exp(scores - log_total)
    probs_low = probs_full.astype(jnp.bfloat16)
    d_values = jnp.einsum('kgql,qkgd->lkd', probs_low.astype(jnp.float32), d_attended.astype(jnp.float32))
    d_probs = jnp.einsum('qkgd,lkd->kgql', d_attended.astype(jnp.float32), value_rows.astype(jnp.float32))
    row_delta = lax.optimization_barrier(jnp.sum(d_attended.astype(jnp.float32) * attended.astype(jnp.float32), axis=-1))
    row_delta = jnp.transpose(row_delta, (1, 2, 0))[..., None]
    d_scores = (probs_full * (d_probs - row_delta) * (1.0 / math.sqrt(HEAD_DIM))).astype(jnp.bfloat16)
    d_queries = jnp.einsum('kgql,lkd->qkgd', d_scores.astype(jnp.float32), key_rows.astype(jnp.float32))
    d_keys = jnp.einsum('kgql,qkgd->lkd', d_scores.astype(jnp.float32), query_rows.astype(jnp.float32))
    d_projected = join_columns(rotate_back(d_queries, cosine[:, None, None, :], sine_table[:, None, None, :]), rotate_back(d_keys, cosine[:, None, :], sine_table[:, None, :]), d_values)
    grad_bias = lax.optimization_barrier(jnp.sum(d_projected, axis=0))
    d_projected_low = d_projected.astype(jnp.bfloat16)
    grad_qkv = jnp.dot(first_normed.T, d_projected_low, preferred_element_type=jnp.float32)
    d_first = jnp.dot(d_projected_low, qkv_w.T, preferred_element_type=jnp.float32)
    d_lower, grad_gain_one = rms_backward(d_first, first_unit, first_scale, gain_pair[0])
    d_hidden = d_mixed + d_lower
    return (d_hidden, (grad_qkv, grad_bias, grad_out, grad_gate_up, grad_down, jnp.stack([grad_gain_one, grad_gain_two])))

def reference(inputs, block_order, cotangent, gains, w_qkv, b_qkv, w_out, w_gate_up, w_down):
    layers = gains.shape[0]
    weights = []
    for layer_index in range(layers):
        weights.append((w_qkv[layer_index].reshape(D, -1), b_qkv[layer_index].reshape(-1), w_out[layer_index].reshape(-1, D), w_gate_up[layer_index], w_down[layer_index], gains[layer_index]))
    offsets = jnp.arange(BLOCK_LEN, dtype=jnp.int32)
    bias_count = b_qkv.shape[1] * b_qkv.shape[2] * b_qkv.shape[3]

    def zero_terms():
        return (jnp.zeros((D, w_qkv.shape[2] * w_qkv.shape[3]), jnp.float32), jnp.zeros((bias_count,), jnp.float32), jnp.zeros((w_out.shape[1] * w_out.shape[2], D), jnp.float32), jnp.zeros(w_gate_up.shape[1:], jnp.float32), jnp.zeros(w_down.shape[1:], jnp.float32), jnp.zeros(gains.shape[1:], jnp.float32))

    def one_sequence(totals, seq_item):
        hidden, slot_order, gradient = seq_item
        positions = (slot_order.astype(jnp.int32)[:, None] * BLOCK_LEN + offsets[None, :]).reshape(-1)
        cosine, sine_table = rotary(positions)
        kept_state = []
        for layer_index in range(layers):
            hidden, saved_state = layer_forward(hidden, positions, cosine, sine_table, weights[layer_index])
            kept_state.append(saved_state)
        new_totals = list(totals)
        for layer_index in reversed(range(layers)):
            gradient, grad_terms = layer_backward(gradient, kept_state[layer_index], positions, cosine, sine_table, weights[layer_index])
            new_totals[layer_index] = tuple((old_term + new_term for old_term, new_term in zip(totals[layer_index], grad_terms)))
        return (tuple(new_totals), (hidden, gradient))
    initial = tuple((zero_terms() for layer_index in range(layers)))
    totals, (outputs, grad_inputs) = lax.scan(one_sequence, initial, (inputs, block_order, cotangent))
    grad_gains = jnp.stack([totals[layer_index][5] for layer_index in range(layers)])
    grad_w_qkv = jnp.stack([totals[layer_index][0].reshape(w_qkv.shape[1:]) for layer_index in range(layers)])
    grad_b_qkv = jnp.stack([totals[layer_index][1].reshape(b_qkv.shape[1:]) for layer_index in range(layers)])
    grad_w_out = jnp.stack([totals[layer_index][2].reshape(w_out.shape[1:]) for layer_index in range(layers)])
    grad_w_gate_up = jnp.stack([totals[layer_index][3] for layer_index in range(layers)])
    grad_w_down = jnp.stack([totals[layer_index][4] for layer_index in range(layers)])
    return (outputs, grad_inputs, grad_gains, grad_w_qkv, grad_b_qkv, grad_w_out, grad_w_gate_up, grad_w_down)
```

```python
import math

import jax
import jax.numpy as jnp
from jax import lax
from jax.experimental import pallas as pl
from jax.experimental.pallas import tpu as pltpu
from jax.sharding import PartitionSpec as P

HD = 64
EPS = 1e-06
ROPE_BASE = 1000000.0
MASKED = -1e30
ROWS = 14
SLOT = 16
DM = 896
DP = 1024
OWNERS = 64
FFB = 640
CH = 256
GRP = ("fsdp", "ctx")
BF = jnp.bfloat16
F32 = jnp.float32
NT = (((1,), (1,)), ((), ()))
TN = (((0,), (0,)), ((), ()))
VMEM_ALL = pl.BlockSpec(memory_space=pltpu.VMEM)
PARAMS = pltpu.CompilerParams(vmem_limit_bytes=56 << 20)


def dot(a, b):
    return jnp.dot(a, b, preferred_element_type=F32)


def dotd(a, b, dims):
    return lax.dot_general(a, b, dims, preferred_element_type=F32)


def low(v):
    return lax.reduce_precision(v, 8, 7)


def selection():
    d = lax.broadcasted_iota(jnp.int32, (DM, DP), 0)
    p = lax.broadcasted_iota(jnp.int32, (DM, DP), 1)
    return ((d // ROWS) * SLOT + d % ROWS == p).astype(BF)


def split3(v):
    hi = low(v)
    rest = v - hi
    mid = low(rest)
    tail = rest - mid
    return jnp.concatenate([hi.astype(BF), mid.astype(BF), tail.astype(BF)], axis=0)


def sum3(v):
    n = v.shape[0] // 3
    return (v[:n] + v[n : 2 * n]) + v[2 * n :]


def pad_features(v, sel):
    return sum3(dot(split3(v), sel))


def unpad_features(v, sel):
    return sum3(dotd(split3(v), sel, NT))


def spread(v, count, axes):
    full = jnp.broadcast_to(v[None], (count,) + v.shape)
    return lax.all_to_all(full, axes, split_axis=0, concat_axis=0, tiled=True)


def swap_tp(v):
    return lax.ppermute(v, "tp", [(0, 1), (1, 0)])


def lanes(shape):
    return lax.broadcasted_iota(jnp.int32, shape, len(shape) - 1)


def half_swap(v, lane):
    return jnp.where(lane % HD < HD // 2, pltpu.roll(v, 96, 1), pltpu.roll(v, 32, 1))


def qkv_kernel(x_ref, w_ref, cos_ref, sin_ref, q_ref, kv_ref, n_ref, g_ref):
    x = x_ref[...]
    scale = lax.rsqrt(jnp.sum(x * x, axis=-1, keepdims=True) * (1.0 / DM) + EPS)
    pick = (
        lax.broadcasted_iota(jnp.int32, (8, 128), 0) + HD
        == lax.broadcasted_iota(jnp.int32, (8, 128), 1)
    ) & (lax.broadcasted_iota(jnp.int32, (8, 128), 0) < 2)
    gain_rows = dotd(jnp.where(pick, 1.0, 0.0).astype(BF), w_ref[:, 512:640], NT)
    g_ref[...] = gain_rows
    wide = lanes(x.shape)
    normed = jnp.where(wide % SLOT == ROWS, 1.0, x * scale * gain_rows[0:1]).astype(BF)
    n_ref[...] = normed
    proj = dot(normed, w_ref[...])
    cosine = cos_ref[...]
    sine = sin_ref[...]
    lane = lanes(cosine.shape)
    left = lane < HD
    rots = []
    for g in range(4):
        v = proj[:, g * 128 : g * 128 + 128]
        rots.append(v * cosine + half_swap(v, lane) * sine)
    for h in range(7):
        r = rots[h // 2]
        if h % 2:
            r = pltpu.roll(r, HD, 1)
        qh = jnp.where(left, r * 0.125, 0.0).astype(BF)
        for s in range(2):
            for b in range(2):
                q_ref[s, b, h * 64 : h * 64 + 64, :] = qh[s * 128 + b * 64 : s * 128 + b * 64 + 64]
    pair = jnp.where(
        left, pltpu.roll(rots[3], HD, 1), pltpu.roll(proj[:, 512:640], HD, 1)
    ).astype(BF)
    for c in range(kv_ref.shape[0]):
        kv_ref[c] = pair


def order_rows(bo_ref, s, kv_ref, kvs):
    for j in range(32):
        at = pl.multiple_of(bo_ref[s, j] * 64, 64)
        kvs[pl.ds(at, 64), :] = kv_ref[j // 2, 0, (j % 2) * 64 : (j % 2) * 64 + 64, :]


def allowed(block, j):
    key = j * CH + lax.broadcasted_iota(jnp.int32, (448, CH), 1)
    query = block * 64 + lax.broadcasted_iota(jnp.int32, (448, CH), 0) % 64
    return key <= query


def attn_fwd_kernel(bo_ref, own_ref, q_ref, kv_ref, att_ref, lse_ref, kvs, sbuf, mbuf, lbuf, obuf):
    s = pl.program_id(0)
    order_rows(bo_ref, s, kv_ref, kvs)
    for b in range(2):
        block = own_ref[s, b]
        count = block // 4 + 1
        q = q_ref[0, b]
        mbuf[...] = jnp.full(mbuf.shape, MASKED, F32)

        def first(j, carry):
            k = kvs[pl.ds(pl.multiple_of(j * CH, CH), CH), :]
            sc = jnp.where(allowed(block, j), dotd(q, k, NT), MASKED)
            sbuf[j] = sc
            mbuf[...] = jnp.maximum(mbuf[...], jnp.maximum(sc[:, :128], sc[:, 128:]))
            return carry

        lax.fori_loop(0, count, first, 0)
        top = jnp.max(mbuf[...], axis=-1, keepdims=True)
        lbuf[...] = jnp.zeros(lbuf.shape, F32)
        obuf[...] = jnp.zeros(obuf.shape, F32)

        def second(j, carry):
            k = kvs[pl.ds(pl.multiple_of(j * CH, CH), CH), :]
            p = jnp.exp(sbuf[j] - top)
            lbuf[...] += p[:, :128] + p[:, 128:]
            obuf[...] += dot(p.astype(BF), k)
            return carry

        lax.fori_loop(0, count, second, 0)
        total = jnp.sum(lbuf[...], axis=-1, keepdims=True)
        lse_ref[0, b] = jnp.broadcast_to(top + jnp.log(total), (448, 128))
        o = obuf[...] / total
        left = lanes((64, 128)) < HD
        for g in range(4):
            even = pltpu.roll(o[g * 128 : g * 128 + 64], HD, 1)
            odd = o[g * 128 + 64 : g * 128 + 128] if g < 3 else jnp.zeros((64, 128), F32)
            att_ref[0, b * 64 : b * 64 + 64, g * 128 : g * 128 + 128] = jnp.where(
                left, even, odd
            ).astype(BF)


def head_rows(ref, b):
    right = lanes((64, 128)) >= HD
    parts = []
    for h in range(7):
        g = h // 2
        v = ref[0, b * 64 : b * 64 + 64, g * 128 : g * 128 + 128].astype(F32)
        if h % 2 == 0:
            v = pltpu.roll(v, HD, 1)
        parts.append(jnp.where(right, v, 0.0))
    return jnp.concatenate(parts, axis=0)


def attn_bwd_kernel(
    bo_ref, own_ref, q_ref, kv_ref, att_ref, do_ref, lse_ref, dq_ref, dkv_ref, kvs, dkvs, dqb
):
    s = pl.program_id(0)
    order_rows(bo_ref, s, kv_ref, kvs)
    dkvs[...] = jnp.zeros(dkvs.shape, F32)
    for b in range(2):
        block = own_ref[s, b]
        count = block // 4 + 1
        q = q_ref[0, b]
        do32 = head_rows(do_ref, b)
        delta = jnp.sum(do32 * head_rows(att_ref, b), axis=-1, keepdims=True)
        do = do32.astype(BF)
        lse = lse_ref[0, b][:, 0:1]
        dqb[...] = jnp.zeros(dqb.shape, F32)

        def step(j, carry):
            at = pl.ds(pl.multiple_of(j * CH, CH), CH)
            k = kvs[at, :]
            p = jnp.where(allowed(block, j), jnp.exp(dotd(q, k, NT) - lse), 0.0)
            ds = (p * (dotd(do, k, NT) - delta)).astype(BF)
            dqb[...] += dot(ds, k)
            dkvs[at, :] += dotd(ds, q, TN) + dotd(p.astype(BF), do, TN)
            return carry

        lax.fori_loop(0, count, step, 0)
        dq_ref[0, b] = dqb[...] * 0.125
    for j in range(32):
        at = pl.multiple_of(bo_ref[s, j] * 64, 64)
        dkv_ref[j // 2, 0, (j % 2) * 64 : (j % 2) * 64 + 64, :] = dkvs[pl.ds(at, 64), :].astype(BF)


def dproj_kernel(dq_ref, dkv_ref, cos_ref, sin_ref, w_ref, dp_ref, dn_ref):
    dkv = dkv_ref[0].astype(F32)
    for c in range(1, dkv_ref.shape[0]):
        dkv = dkv + dkv_ref[c].astype(F32)
    cosine = cos_ref[...]
    sine = sin_ref[...]
    lane = lanes(cosine.shape)
    left = lane < HD

    def head(h):
        return jnp.concatenate(
            [dq_ref[s, b, h * 64 : h * 64 + 64, :] for s in range(2) for b in range(2)], axis=0
        )

    for g in range(4):
        odd = head(2 * g + 1) if g < 3 else dkv
        u = jnp.where(left, head(2 * g), pltpu.roll(odd, HD, 1))
        dp_ref[:, g * 128 : g * 128 + 128] = (u * cosine - half_swap(u, lane) * sine).astype(BF)
    dp_ref[:, 512:640] = jnp.where(left, pltpu.roll(dkv, HD, 1), 0.0).astype(BF)
    dn_ref[...] = dotd(dp_ref[...], w_ref[...], NT)


def mlp_kernel(n_ref, dm_ref, w_ref, act_ref, dg_ref, du_ref, dn_ref, out_ref):
    n = n_ref[...]
    gate = dot(n, w_ref[:, 0:FFB])
    up = dot(n, w_ref[:, FFB : 2 * FFB])
    dact = dot(dm_ref[...], w_ref[:, 2 * FFB : 3 * FFB])
    sg = 1.0 / (1.0 + jnp.exp(-gate))
    silu = gate * sg
    act = (silu * up).astype(BF)
    dg = (dact * up * sg * (1.0 + gate * (1.0 - sg))).astype(BF)
    du = (dact * silu).astype(BF)
    act_ref[...] = act
    dg_ref[...] = dg
    du_ref[...] = du
    dn_ref[...] = (dotd(dg, w_ref[:, 0:FFB], NT) + dotd(du, w_ref[:, FFB : 2 * FFB], NT)).astype(BF)
    out_ref[...] = dotd(act, w_ref[:, 2 * FFB : 3 * FFB], NT).astype(BF)


def wgrad_kernel(
    n0, n1, m0, m1, a0, a1, g0, g1, u0, u1, da_ref, att_ref, out_ref
):
    out_ref[:, 0:FFB] = (dotd(n0[...], g0[...], TN) + dotd(n1[...], g1[...], TN)).astype(BF)
    out_ref[:, FFB : 2 * FFB] = (dotd(n0[...], u0[...], TN) + dotd(n1[...], u1[...], TN)).astype(BF)
    out_ref[:, 2 * FFB : 3 * FFB] = (
        dotd(m0[...], a0[...], TN) + dotd(m1[...], a1[...], TN)
    ).astype(BF)
    out_ref[:, 3 * FFB :] = dotd(da_ref[...], att_ref[...], TN).astype(BF)


def call(kernel, outs, *args, name=None):
    return pl.pallas_call(
        kernel,
        out_shape=[jax.ShapeDtypeStruct(s, t) for s, t in outs],
        in_specs=[VMEM_ALL] * len(args),
        out_specs=[VMEM_ALL] * len(outs),
        compiler_params=PARAMS,
        name=name,
    )(*args)


def attn_fwd(bo, own, q, kv):
    return pl.pallas_call(
        attn_fwd_kernel,
        out_shape=[
            jax.ShapeDtypeStruct((2, 128, 512), BF),
            jax.ShapeDtypeStruct((2, 2, 448, 128), F32),
        ],
        grid_spec=pltpu.PrefetchScalarGridSpec(
            num_scalar_prefetch=2,
            grid=(2,),
            in_specs=[
                pl.BlockSpec((1, 2, 448, 128), lambda s, *_: (s, 0, 0, 0)),
                pl.BlockSpec((16, 1, 128, 128), lambda s, *_: (0, s, 0, 0)),
            ],
            out_specs=[
                pl.BlockSpec((1, 128, 512), lambda s, *_: (s, 0, 0)),
                pl.BlockSpec((1, 2, 448, 128), lambda s, *_: (s, 0, 0, 0)),
            ],
            scratch_shapes=[
                pltpu.VMEM((2048, 128), BF),
                pltpu.VMEM((8, 448, CH), F32),
                pltpu.VMEM((448, 128), F32),
                pltpu.VMEM((448, 128), F32),
                pltpu.VMEM((448, 128), F32),
            ],
        ),
        compiler_params=PARAMS,
        name="attn_fwd",
    )(bo, own, q, kv)


def attn_bwd(bo, own, q, kv, att, datt, lse):
    per_seq = pl.BlockSpec((1, 2, 448, 128), lambda s, *_: (s, 0, 0, 0))
    tokens = pl.BlockSpec((1, 128, 512), lambda s, *_: (s, 0, 0))
    pairs = pl.BlockSpec((16, 1, 128, 128), lambda s, *_: (0, s, 0, 0))
    return pl.pallas_call(
        attn_bwd_kernel,
        out_shape=[
            jax.ShapeDtypeStruct((2, 2, 448, 128), F32),
            jax.ShapeDtypeStruct((16, 2, 128, 128), BF),
        ],
        grid_spec=pltpu.PrefetchScalarGridSpec(
            num_scalar_prefetch=2,
            grid=(2,),
            in_specs=[per_seq, pairs, tokens, tokens, per_seq],
            out_specs=[per_seq, pairs],
            scratch_shapes=[
                pltpu.VMEM((2048, 128), BF),
                pltpu.VMEM((2048, 128), F32),
                pltpu.VMEM((448, 128), F32),
            ],
        ),
        compiler_params=PARAMS,
        name="attn_bwd",
    )(bo, own, q, kv, att, datt, lse)


def mlp(n, dm, w2):
    tok = pl.BlockSpec((256, DP), lambda i: (i, 0))
    hid = pl.BlockSpec((256, FFB), lambda i: (i, 0))
    return pl.pallas_call(
        mlp_kernel,
        out_shape=[jax.ShapeDtypeStruct((512, FFB), BF)] * 3
        + [jax.ShapeDtypeStruct((512, DP), BF)] * 2,
        grid=(2,),
        in_specs=[
            tok,
            tok,
            pl.BlockSpec((DP, 3 * FFB), lambda i: (0, 0), pipeline_mode=pl.Buffered(1)),
        ],
        out_specs=[hid, hid, hid, tok, tok],
        compiler_params=PARAMS,
        name="mlp",
    )(n, dm, w2)


def wgrads(n0, n1, m0, m1, first, second, da, att):
    feat = pl.BlockSpec((512, 256), lambda i: (0, i))
    hid = pl.BlockSpec((512, FFB), lambda i: (0, 0))
    args = [n0, n1, m0, m1, first[0], second[0], first[1], second[1], first[2], second[2], da, att]
    return pl.pallas_call(
        wgrad_kernel,
        out_shape=jax.ShapeDtypeStruct((DP, 3 * FFB + 512), BF),
        grid=(4,),
        in_specs=[feat] * 4
        + [hid] * 6
        + [
            pl.BlockSpec((256, 256), lambda i: (0, i)),
            pl.BlockSpec((256, 512), lambda i: (0, 0)),
        ],
        out_specs=pl.BlockSpec((256, 3 * FFB + 512), lambda i: (i, 0)),
        compiler_params=PARAMS,
        name="wgrad",
    )(*args)


def rms(v):
    scale = lax.rsqrt(jnp.sum(v * v, axis=-1, keepdims=True) * (1.0 / DM) + EPS)
    return v * scale, scale


def rms_back(dn, unit, scale, gain):
    e = dn * gain
    mean = jnp.sum(e * unit, axis=-1, keepdims=True) * (1.0 / DM)
    return scale * (e - unit * mean), jnp.sum(dn * unit, axis=0)


def pick(v, index):
    return lax.dynamic_index_in_dim(v, index, 0, keepdims=False)


def both(own, other, t):
    return jnp.stack([jnp.where(t == 0, own, other), jnp.where(t == 0, other, own)])


def scatter_fsdp(own, other):
    pair = own.astype(F32) + swap_tp(other).astype(F32)
    got = lax.all_to_all(
        pair.astype(BF).reshape(4, 128, DP), "fsdp", split_axis=0, concat_axis=0, tiled=True
    )
    return jnp.sum(got.astype(F32), axis=0)


def body(inputs, block_order, cotangent, gains, w_qkv, b_qkv, w_out, w_gate_up, w_down):
    seqs, toks, width = inputs.shape
    ctx = lax.axis_index("ctx")
    t = lax.axis_index("tp")
    owner = lax.axis_index("fsdp") * 16 + ctx
    sel = selection()

    bias_row = jnp.where(jnp.arange(HD) == owner, b_qkv[0, 0], jnp.zeros((), BF)).reshape(1, 9 * HD)
    patch1 = jnp.concatenate(
        [
            jnp.concatenate([w_qkv[0, :, 0, :], bias_row, jnp.zeros((1, 9 * HD), BF)], axis=0),
            jnp.pad(gains[0].T, ((0, 2), (0, HD - 2))),
        ],
        axis=1,
    )
    w1 = spread(patch1, OWNERS, GRP).reshape(DP, 640)

    tall = jnp.pad(w_gate_up[0], ((0, 2), (0, 0), (0, 4 * FFB - 2432)))
    gate_parts = tall[:, 0].reshape(SLOT, 4, FFB).transpose(1, 0, 2)
    up_parts = tall[:, 1].reshape(SLOT, 4, FFB).transpose(1, 0, 2)
    down_parts = (
        jnp.pad(w_down[0].T, ((0, 2), (0, 4 * FFB - 2432)))
        .reshape(SLOT, 4, FFB)
        .transpose(1, 0, 2)
    )
    out_part = jnp.broadcast_to(jnp.pad(w_out[0, 0].T, ((0, 2), (0, 64)))[None], (4, SLOT, 512))
    patch2 = jnp.concatenate([gate_parts, up_parts, down_parts, out_part], axis=2)
    send2 = jnp.broadcast_to(patch2[:, None], (4, 16, SLOT, 3 * FFB + 512)).reshape(
        OWNERS, SLOT, 3 * FFB + 512
    )
    w2 = lax.all_to_all(send2, GRP, split_axis=0, concat_axis=0, tiled=True).reshape(
        DP, 3 * FFB + 512
    )
    wo = w2[:, 3 * FFB :]

    own = lax.dynamic_slice_in_dim(block_order, 2 * ctx, 2, 1)
    pos = (own[:, :, None] * 64 + jnp.arange(64, dtype=jnp.int32)).reshape(seqs * toks, 1)
    lane = lax.broadcasted_iota(jnp.int32, (1, 128), 1)
    freq = jnp.exp((lane % 32).astype(F32) * (-2.0 * math.log(ROPE_BASE) / HD))
    angle = pos.astype(F32) * freq
    cosine = jnp.cos(angle)
    sine = jnp.where(lane % HD < HD // 2, -1.0, 1.0) * jnp.sin(angle)

    x = pad_features(inputs.reshape(seqs * toks, width), sel)
    g = pad_features(cotangent.reshape(seqs * toks, width), sel)
    xh = pick(x.reshape(2, 128, DP), t)
    gh = pick(g.reshape(2, 128, DP), t)
    m0 = spread(gh.astype(BF), 4, "fsdp").reshape(512, DP)
    m1 = swap_tp(m0)

    q, pairs, normed1, gain_rows = call(
        qkv_kernel,
        [((2, 2, 448, 128), BF), ((16, 256, 128), BF), ((256, DP), BF), ((8, DP), F32)],
        x, w1, cosine, sine, name="qkv",
    )
    gain1 = gain_rows[0:1]
    gain2 = gain_rows[1:2]
    kv = lax.all_to_all(pairs, "ctx", split_axis=0, concat_axis=0, tiled=True).reshape(
        16, 2, 128, 128
    )
    att, lse = attn_fwd(block_order, own, q, kv)
    att2 = att.reshape(256, 512)
    mixed = dotd(att2, wo, NT).reshape(2, 128, DP)
    h2 = xh + (pick(mixed, t) + swap_tp(pick(mixed, 1 - t).astype(BF)).astype(F32))
    unit2, scale2 = rms(h2)
    n0 = spread((unit2 * gain2).astype(BF), 4, "fsdp").reshape(512, DP)
    n1 = swap_tp(n0)
    first = mlp(n0, m0, w2)
    second = mlp(n1, m1, w2)

    dn2 = scatter_fsdp(first[3], second[3])
    back2, gg2 = rms_back(dn2, unit2, scale2, gain2)
    g2 = gh + back2
    dah = g2.astype(BF)
    da = both(dah, swap_tp(dah), t).reshape(256, DP)
    datt = dot(da, wo).astype(BF).reshape(2, 128, 512)
    big = wgrads(n0, n1, m0, m1, first, second, da, att2).reshape(OWNERS, SLOT, 3 * FFB + 512)
    big = lax.all_to_all(big, GRP, split_axis=0, concat_axis=0, tiled=True)

    dq, dkv = attn_bwd(block_order, own, q, kv, att, datt, lse)
    dkv = lax.all_to_all(dkv, "ctx", split_axis=0, concat_axis=0, tiled=True).reshape(16, 256, 128)
    dproj, dn1 = call(
        dproj_kernel, [((256, 640), BF), ((256, DP), F32)], dq, dkv, cosine, sine, w1, name="dproj"
    )
    dn1 = dn1.reshape(2, 128, DP)
    dn1h = pick(dn1, t) + swap_tp(pick(dn1, 1 - t).astype(BF)).astype(F32)
    unit1, scale1 = rms(xh)
    back1, gg1 = rms_back(dn1h, unit1, scale1, gain1)
    gin = unpad_features(g2 + back1, sel)
    grad_inputs = both(gin, swap_tp(gin), t)

    place = (jnp.arange(640)[None, :] == 576 + jnp.arange(2)[:, None]).astype(BF)
    gq = dotd(normed1, dproj, TN) + dotd(jnp.stack([gg1, gg2]).astype(BF), place, TN)
    gq = lax.all_to_all(
        gq.astype(BF).reshape(OWNERS, SLOT, 640), GRP, split_axis=0, concat_axis=0, tiled=True
    )

    outh = h2 + scatter_fsdp(first[4], second[4])
    outh = unpad_features(outh, sel)
    outputs = both(outh, swap_tp(outh), t)

    big = jnp.sum(big.reshape(4, 16, SLOT, 3 * FFB + 512).astype(F32), axis=1)
    hidden = big[:, :ROWS, : 3 * FFB].transpose(1, 0, 2)

    def columns(k):
        return hidden[:, :, k * FFB : k * FFB + FFB].reshape(ROWS, 4 * FFB)[:, :2432]

    grad_gate_up = jnp.stack([columns(0), columns(1)], axis=1)[None]
    grad_down = columns(2).T[None]
    grad_out = jnp.sum(big[:, :ROWS, 3 * FFB : 3 * FFB + 448], axis=0).T[None, None]
    gq = jnp.sum(gq.astype(F32), axis=0)
    grad_qkv = gq[None, :ROWS, None, :576]
    grad_bias = lax.dynamic_slice_in_dim(gq[ROWS, :576].reshape(9, HD), owner, 1, 1)[None, None]
    gg = gq[:ROWS, 576:578].T
    grad_gains = (gg + swap_tp(gg))[None]
    return (outputs, grad_inputs, grad_gains, grad_qkv, grad_bias, grad_out, grad_gate_up, grad_down)


def solution(mesh):
    in_specs = (
        P("fsdp", "ctx", None),
        P("fsdp", None),
        P("fsdp", "ctx", None),
        P(None, None, ("fsdp", "ctx")),
        P(None, ("fsdp", "ctx"), "tp", None),
        P(None, "tp", None, ("fsdp", "ctx")),
        P(None, "tp", None, ("fsdp", "ctx")),
        P(None, ("fsdp", "ctx"), None, "tp"),
        P(None, "tp", ("fsdp", "ctx")),
    )
    out_specs = (
        P("fsdp", "ctx", None),
        P("fsdp", "ctx", None),
        P(None, None, ("fsdp", "ctx")),
        P(None, ("fsdp", "ctx"), "tp", None),
        P(None, "tp", None, ("fsdp", "ctx")),
        P(None, "tp", None, ("fsdp", "ctx")),
        P(None, ("fsdp", "ctx"), None, "tp"),
        P(None, "tp", ("fsdp", "ctx")),
    )
    return jax.shard_map(body, mesh=mesh, in_specs=in_specs, out_specs=out_specs, check_vma=False)
```

```python
import math

import jax
import jax.numpy as jnp
from jax import lax
from jax.experimental import pallas as pl
from jax.experimental.pallas import tpu as pltpu
from jax.sharding import PartitionSpec as P

HD = 64
EPS = 1e-06
ROPE_BASE = 1000000.0
MASKED = -1e30
ROWS = 14
SLOT = 16
DM = 896
DP = 1024
FFB = 640
CH = 256
BF = jnp.bfloat16
F32 = jnp.float32
NT = (((1,), (1,)), ((), ()))
TN = (((0,), (0,)), ((), ()))
VMEM_ALL = pl.BlockSpec(memory_space=pltpu.VMEM)
PARAMS = pltpu.CompilerParams(vmem_limit_bytes=56 << 20)


def dot(a, b):
    return jnp.dot(a, b, preferred_element_type=F32)


def dotd(a, b, dims):
    return lax.dot_general(a, b, dims, preferred_element_type=F32)


def low(v):
    return lax.reduce_precision(v, 8, 7)


def selection(z, x):
    d = lax.broadcasted_iota(jnp.int32, (DM, DP), 0)
    p = lax.broadcasted_iota(jnp.int32, (1, DP), 1)
    step = p // 64
    owner = (p // SLOT % 4) * 16 + ((z - step // 4) % 4) * 4 + (x - step % 4) % 4
    feature = jnp.where(p % SLOT < ROWS, owner * ROWS + p % SLOT, -1)
    return (d == feature).astype(BF)


def split3(v):
    hi = low(v)
    rest = v - hi
    mid = low(rest)
    tail = rest - mid
    return jnp.concatenate([hi.astype(BF), mid.astype(BF), tail.astype(BF)], axis=0)


def sum3(v):
    n = v.shape[0] // 3
    return (v[:n] + v[n : 2 * n]) + v[2 * n :]


def pad_features(v, sel):
    return sum3(dot(split3(v), sel))


def unpad_features(v, sel):
    return sum3(dotd(split3(v), sel, NT))


FSDP_STEPS = (0, 1, 3, 2)


def ring(v, k):
    return lax.ppermute(v, "fsdp", [(i, (i + k) % 4) for i in range(4)]) if k % 4 else v


def shift(v, step, sign):
    dz, dx = sign * (step // 4), sign * (step % 4)
    if step == 0:
        return v
    return lax.ppermute(
        v, "ctx", [(c, (c // 4 + dz) % 4 * 4 + (c % 4 + dx) % 4) for c in range(16)]
    )


def ctx_gather(v):
    return [shift(v, r, 1) for r in range(16)]


def ctx_scatter(parts):
    return [shift(v, r, -1) for r, v in enumerate(parts)]


def fsdp_gather(v):
    return [ring(v, k) for k in FSDP_STEPS]


def fsdp_place(parts, f):
    out = jnp.zeros((4,) + parts[0].shape, parts[0].dtype)
    for k, v in zip(FSDP_STEPS, parts):
        out = lax.dynamic_update_index_in_dim(out, v, (f - k) % 4, 0)
    return out


def fsdp_exchange(v, f):
    return [ring(pick(v, (f + k) % 4), k) for k in FSDP_STEPS]


def total(parts):
    out = parts[0].astype(F32)
    for v in parts[1:]:
        out = out + v.astype(F32)
    return out


def swap_tp(v):
    return lax.ppermute(v, "tp", [(0, 1), (1, 0)])


def lanes(shape):
    return lax.broadcasted_iota(jnp.int32, shape, len(shape) - 1)


def half_swap(v, lane):
    return jnp.where(lane % HD < HD // 2, pltpu.roll(v, 96, 1), pltpu.roll(v, 32, 1))


def qkv_kernel(x_ref, cos_ref, sin_ref, *refs):
    pieces = refs[:16]
    q_ref, kv_ref, n_ref, g_ref, w_ref, wo_ref = refs[16:]
    for r in range(16):
        w_ref[r * 64 : r * 64 + 64, :] = pieces[r][:, :640]
        wo_ref[r * 64 : r * 64 + 64, :] = pieces[r][:, 640:]
    x = x_ref[...]
    scale = lax.rsqrt(jnp.sum(x * x, axis=-1, keepdims=True) * (1.0 / DM) + EPS)
    pick = (
        lax.broadcasted_iota(jnp.int32, (8, 128), 0) + HD
        == lax.broadcasted_iota(jnp.int32, (8, 128), 1)
    ) & (lax.broadcasted_iota(jnp.int32, (8, 128), 0) < 2)
    gain_rows = dotd(jnp.where(pick, 1.0, 0.0).astype(BF), w_ref[:, 512:640], NT)
    g_ref[...] = gain_rows
    wide = lanes(x.shape)
    normed = jnp.where(wide % SLOT == ROWS, 1.0, x * scale * gain_rows[0:1]).astype(BF)
    n_ref[...] = normed
    proj = dot(normed, w_ref[...])
    cosine = cos_ref[...]
    sine = sin_ref[...]
    lane = lanes(cosine.shape)
    left = lane < HD
    rots = []
    for g in range(4):
        v = proj[:, g * 128 : g * 128 + 128]
        rots.append(v * cosine + half_swap(v, lane) * sine)
    for h in range(7):
        r = rots[h // 2]
        if h % 2:
            r = pltpu.roll(r, HD, 1)
        qh = jnp.where(left, r * 0.125, 0.0).astype(BF)
        for s in range(2):
            for b in range(2):
                q_ref[s, b, h * 64 : h * 64 + 64, :] = qh[s * 128 + b * 64 : s * 128 + b * 64 + 64]
    kv_ref[...] = jnp.where(
        left, pltpu.roll(rots[3], HD, 1), pltpu.roll(proj[:, 512:640], HD, 1)
    ).astype(BF)


def row_of(bo_ref, zx_ref, s, j):
    step = j // 2
    c = ((zx_ref[0] + 4 - step // 4) & 3) * 4 + ((zx_ref[1] + 4 - step % 4) & 3)
    return pl.multiple_of(bo_ref[s, c * 2 + j % 2] * 64, 64)


def order_rows(bo_ref, zx_ref, s, kv_refs, kvs):
    for j in range(32):
        at = row_of(bo_ref, zx_ref, s, j)
        kvs[pl.ds(at, 64), :] = kv_refs[j // 2][(j % 2) * 64 : (j % 2) * 64 + 64, :]


def allowed(block, j):
    key = j * CH + lax.broadcasted_iota(jnp.int32, (448, CH), 1)
    query = block * 64 + lax.broadcasted_iota(jnp.int32, (448, CH), 0) % 64
    return key <= query


def attn_fwd_kernel(bo_ref, own_ref, zx_ref, q_ref, *refs):
    att_ref, lse_ref, kvs, sbuf, mbuf, lbuf, obuf = refs[16:]
    s = pl.program_id(0)
    order_rows(bo_ref, zx_ref, s, refs[:16], kvs)
    for b in range(2):
        block = own_ref[s, b]
        count = block // 4 + 1
        q = q_ref[0, b]
        mbuf[...] = jnp.full(mbuf.shape, MASKED, F32)

        def first(j, carry):
            k = kvs[pl.ds(pl.multiple_of(j * CH, CH), CH), :]
            sc = jnp.where(allowed(block, j), dotd(q, k, NT), MASKED)
            sbuf[j] = sc
            mbuf[...] = jnp.maximum(mbuf[...], jnp.maximum(sc[:, :128], sc[:, 128:]))
            return carry

        lax.fori_loop(0, count, first, 0)
        top = jnp.max(mbuf[...], axis=-1, keepdims=True)
        lbuf[...] = jnp.zeros(lbuf.shape, F32)
        obuf[...] = jnp.zeros(obuf.shape, F32)

        def second(j, carry):
            k = kvs[pl.ds(pl.multiple_of(j * CH, CH), CH), :]
            p = jnp.exp(sbuf[j] - top)
            lbuf[...] += p[:, :128] + p[:, 128:]
            obuf[...] += dot(p.astype(BF), k)
            return carry

        lax.fori_loop(0, count, second, 0)
        norm = jnp.sum(lbuf[...], axis=-1, keepdims=True)
        lse_ref[0, b] = jnp.broadcast_to(top + jnp.log(norm), (448, 128))
        o = obuf[...] / norm
        left = lanes((64, 128)) < HD
        for g in range(4):
            even = pltpu.roll(o[g * 128 : g * 128 + 64], HD, 1)
            odd = o[g * 128 + 64 : g * 128 + 128] if g < 3 else jnp.zeros((64, 128), F32)
            att_ref[0, b * 64 : b * 64 + 64, g * 128 : g * 128 + 128] = jnp.where(
                left, even, odd
            ).astype(BF)


def head_rows(ref, b):
    right = lanes((64, 128)) >= HD
    parts = []
    for h in range(7):
        g = h // 2
        v = ref[0, b * 64 : b * 64 + 64, g * 128 : g * 128 + 128].astype(F32)
        if h % 2 == 0:
            v = pltpu.roll(v, HD, 1)
        parts.append(jnp.where(right, v, 0.0))
    return jnp.concatenate(parts, axis=0)


def attn_bwd_kernel(bo_ref, own_ref, zx_ref, q_ref, att_ref, do_ref, lse_ref, *refs):
    dq_ref = refs[16]
    dkv_refs = refs[17:33]
    kvs, dkvs, dqb = refs[33:]
    s = pl.program_id(0)
    order_rows(bo_ref, zx_ref, s, refs[:16], kvs)
    dkvs[...] = jnp.zeros(dkvs.shape, F32)
    for b in range(2):
        block = own_ref[s, b]
        count = block // 4 + 1
        q = q_ref[0, b]
        do32 = head_rows(do_ref, b)
        delta = jnp.sum(do32 * head_rows(att_ref, b), axis=-1, keepdims=True)
        do = do32.astype(BF)
        lse = lse_ref[0, b][:, 0:1]
        dqb[...] = jnp.zeros(dqb.shape, F32)

        def step(j, carry):
            at = pl.ds(pl.multiple_of(j * CH, CH), CH)
            k = kvs[at, :]
            p = jnp.where(allowed(block, j), jnp.exp(dotd(q, k, NT) - lse), 0.0)
            ds = (p * (dotd(do, k, NT) - delta)).astype(BF)
            dqb[...] += dot(ds, k)
            dkvs[at, :] += dotd(ds, q, TN) + dotd(p.astype(BF), do, TN)
            return carry

        lax.fori_loop(0, count, step, 0)
        dq_ref[0, b] = dqb[...] * 0.125
    for j in range(32):
        at = row_of(bo_ref, zx_ref, s, j)
        dkv_refs[j // 2][(j % 2) * 64 : (j % 2) * 64 + 64, :] = dkvs[pl.ds(at, 64), :].astype(BF)


def dproj_kernel(dq_ref, cos_ref, sin_ref, w_ref, *refs):
    dp_ref, dn_ref = refs[16:]
    dkv = total([r[...] for r in refs[:16]])
    cosine = cos_ref[...]
    sine = sin_ref[...]
    lane = lanes(cosine.shape)
    left = lane < HD

    def head(h):
        return jnp.concatenate(
            [dq_ref[s, b, h * 64 : h * 64 + 64, :] for s in range(2) for b in range(2)], axis=0
        )

    for g in range(4):
        odd = head(2 * g + 1) if g < 3 else dkv
        u = jnp.where(left, head(2 * g), pltpu.roll(odd, HD, 1))
        dp_ref[:, g * 128 : g * 128 + 128] = (u * cosine - half_swap(u, lane) * sine).astype(BF)
    dp_ref[:, 512:640] = jnp.where(left, pltpu.roll(dkv, HD, 1), 0.0).astype(BF)
    dn_ref[...] = dotd(dp_ref[...], w_ref[...], NT)


def mlp_kernel(n_ref, dm_ref, w_ref, act_ref, dg_ref, du_ref, dn_ref, out_ref):
    n = n_ref[...]
    gate = dot(n, w_ref[:, 0:FFB])
    up = dot(n, w_ref[:, FFB : 2 * FFB])
    dact = dot(dm_ref[...], w_ref[:, 2 * FFB : 3 * FFB])
    sg = 1.0 / (1.0 + jnp.exp(-gate))
    silu = gate * sg
    act = (silu * up).astype(BF)
    dg = (dact * up * sg * (1.0 + gate * (1.0 - sg))).astype(BF)
    du = (dact * silu).astype(BF)
    act_ref[...] = act
    dg_ref[...] = dg
    du_ref[...] = du
    dn_ref[...] = (dotd(dg, w_ref[:, 0:FFB], NT) + dotd(du, w_ref[:, FFB : 2 * FFB], NT)).astype(BF)
    out_ref[...] = dotd(act, w_ref[:, 2 * FFB : 3 * FFB], NT).astype(BF)


def wgrad_kernel(
    n0, n1, m0, m1, a0, a1, g0, g1, u0, u1, out_ref
):
    out_ref[:, 0:FFB] = (dotd(n0[...], g0[...], TN) + dotd(n1[...], g1[...], TN)).astype(BF)
    out_ref[:, FFB : 2 * FFB] = (dotd(n0[...], u0[...], TN) + dotd(n1[...], u1[...], TN)).astype(BF)
    out_ref[:, 2 * FFB : 3 * FFB] = (
        dotd(m0[...], a0[...], TN) + dotd(m1[...], a1[...], TN)
    ).astype(BF)


def call(kernel, outs, *args, name=None):
    return pl.pallas_call(
        kernel,
        out_shape=[jax.ShapeDtypeStruct(s, t) for s, t in outs],
        in_specs=[VMEM_ALL] * len(args),
        out_specs=[VMEM_ALL] * len(outs),
        compiler_params=PARAMS,
        name=name,
    )(*args)


def attn_fwd(bo, own, zx, q, kv):
    return pl.pallas_call(
        attn_fwd_kernel,
        out_shape=[
            jax.ShapeDtypeStruct((2, 128, 512), BF),
            jax.ShapeDtypeStruct((2, 2, 448, 128), F32),
        ],
        grid_spec=pltpu.PrefetchScalarGridSpec(
            num_scalar_prefetch=3,
            grid=(2,),
            in_specs=[pl.BlockSpec((1, 2, 448, 128), lambda s, *_: (s, 0, 0, 0))]
            + [pl.BlockSpec((128, 128), lambda s, *_: (s, 0))] * 16,
            out_specs=[
                pl.BlockSpec((1, 128, 512), lambda s, *_: (s, 0, 0)),
                pl.BlockSpec((1, 2, 448, 128), lambda s, *_: (s, 0, 0, 0)),
            ],
            scratch_shapes=[
                pltpu.VMEM((2048, 128), BF),
                pltpu.VMEM((8, 448, CH), F32),
                pltpu.VMEM((448, 128), F32),
                pltpu.VMEM((448, 128), F32),
                pltpu.VMEM((448, 128), F32),
            ],
        ),
        compiler_params=PARAMS,
        name="attn_fwd",
    )(bo, own, zx, q, *kv)


def attn_bwd(bo, own, zx, q, kv, att, datt, lse):
    per_seq = pl.BlockSpec((1, 2, 448, 128), lambda s, *_: (s, 0, 0, 0))
    tokens = pl.BlockSpec((1, 128, 512), lambda s, *_: (s, 0, 0))
    pairs = [pl.BlockSpec((128, 128), lambda s, *_: (s, 0))] * 16
    return pl.pallas_call(
        attn_bwd_kernel,
        out_shape=[
            jax.ShapeDtypeStruct((2, 2, 448, 128), F32),
        ]
        + [jax.ShapeDtypeStruct((256, 128), BF)] * 16,
        grid_spec=pltpu.PrefetchScalarGridSpec(
            num_scalar_prefetch=3,
            grid=(2,),
            in_specs=[per_seq, tokens, tokens, per_seq] + pairs,
            out_specs=[per_seq] + pairs,
            scratch_shapes=[
                pltpu.VMEM((2048, 128), BF),
                pltpu.VMEM((2048, 128), F32),
                pltpu.VMEM((448, 128), F32),
            ],
        ),
        compiler_params=PARAMS,
        name="attn_bwd",
    )(bo, own, zx, q, att, datt, lse, *kv)


def mlp(n, dm, w2):
    tok = pl.BlockSpec((256, DP), lambda i: (i, 0))
    hid = pl.BlockSpec((256, FFB), lambda i: (i, 0))
    return pl.pallas_call(
        mlp_kernel,
        out_shape=[jax.ShapeDtypeStruct((512, FFB), BF)] * 3
        + [jax.ShapeDtypeStruct((512, DP), BF)] * 2,
        grid=(2,),
        in_specs=[
            tok,
            tok,
            pl.BlockSpec((DP, 3 * FFB), lambda i: (0, 0), pipeline_mode=pl.Buffered(1)),
        ],
        out_specs=[hid, hid, hid, tok, tok],
        compiler_params=PARAMS,
        name="mlp",
    )(n, dm, w2)


def wgrads(n0, n1, m0, m1, first, second):
    feat = pl.BlockSpec((512, 256), lambda i: (0, i))
    hid = pl.BlockSpec((512, FFB), lambda i: (0, 0))
    args = [n0, n1, m0, m1, first[0], second[0], first[1], second[1], first[2], second[2]]
    return pl.pallas_call(
        wgrad_kernel,
        out_shape=jax.ShapeDtypeStruct((DP, 3 * FFB), BF),
        grid=(4,),
        in_specs=[feat] * 4 + [hid] * 6,
        out_specs=pl.BlockSpec((256, 3 * FFB), lambda i: (i, 0)),
        compiler_params=PARAMS,
        name="wgrad",
    )(*args)


def rms(v):
    scale = lax.rsqrt(jnp.sum(v * v, axis=-1, keepdims=True) * (1.0 / DM) + EPS)
    return v * scale, scale


def rms_back(dn, unit, scale, gain):
    e = dn * gain
    mean = jnp.sum(e * unit, axis=-1, keepdims=True) * (1.0 / DM)
    return scale * (e - unit * mean), jnp.sum(dn * unit, axis=0)


def pick(v, index):
    return lax.dynamic_index_in_dim(v, index, 0, keepdims=False)


def both(own, other, t):
    return jnp.stack([jnp.where(t == 0, own, other), jnp.where(t == 0, other, own)])


def scatter_tokens(own, other):
    pair = (own.astype(F32) + swap_tp(other).astype(F32)).astype(BF).reshape(4, 128, DP)
    return total([ring(pair[i], -k) for i, k in enumerate(FSDP_STEPS)])


def row_blocks(v):
    return [v[r * 64 : r * 64 + 64] for r in range(16)]


def body(inputs, block_order, cotangent, gains, w_qkv, b_qkv, w_out, w_gate_up, w_down):
    seqs, toks, width = inputs.shape
    ctx = lax.axis_index("ctx")
    t = lax.axis_index("tp")
    f = lax.axis_index("fsdp")
    owner = f * 16 + ctx
    z, x_at = ctx // 4, ctx % 4
    zx = jnp.stack([z, x_at]).astype(jnp.int32)
    sel = selection(z, x_at)

    bias_row = jnp.where(jnp.arange(HD) == owner, b_qkv[0, 0], jnp.zeros((), BF)).reshape(1, 9 * HD)
    patch1 = jnp.concatenate(
        [
            jnp.concatenate([w_qkv[0, :, 0, :], bias_row, jnp.zeros((1, 9 * HD), BF)], axis=0),
            jnp.pad(gains[0].T, ((0, 2), (0, HD - 2))),
            jnp.pad(w_out[0, 0].T, ((0, 2), (0, 64))),
        ],
        axis=1,
    )
    w1_pieces = ctx_gather(fsdp_place(fsdp_gather(patch1), f).reshape(64, 1152))

    tall = jnp.pad(w_gate_up[0], ((0, 2), (0, 0), (0, 4 * FFB - 2432)))
    gate_parts = tall[:, 0].reshape(SLOT, 4, FFB).transpose(1, 0, 2)
    up_parts = tall[:, 1].reshape(SLOT, 4, FFB).transpose(1, 0, 2)
    down_parts = (
        jnp.pad(w_down[0].T, ((0, 2), (0, 4 * FFB - 2432)))
        .reshape(SLOT, 4, FFB)
        .transpose(1, 0, 2)
    )
    patch2 = jnp.concatenate([gate_parts, up_parts, down_parts], axis=2)
    w2_own = fsdp_place(fsdp_exchange(patch2, f), f).reshape(64, 3 * FFB)

    own = lax.dynamic_slice_in_dim(block_order, 2 * ctx, 2, 1)
    pos = (own[:, :, None] * 64 + jnp.arange(64, dtype=jnp.int32)).reshape(seqs * toks, 1)
    lane = lax.broadcasted_iota(jnp.int32, (1, 128), 1)
    freq = jnp.exp((lane % 32).astype(F32) * (-2.0 * math.log(ROPE_BASE) / HD))
    angle = pos.astype(F32) * freq
    cosine = jnp.cos(angle)
    sine = jnp.where(lane % HD < HD // 2, -1.0, 1.0) * jnp.sin(angle)

    x = pad_features(inputs.reshape(seqs * toks, width), sel)
    g = pad_features(cotangent.reshape(seqs * toks, width), sel)
    xh = pick(x.reshape(2, 128, DP), t)
    gh = pick(g.reshape(2, 128, DP), t)
    m0 = jnp.concatenate(fsdp_gather(gh.astype(BF)), axis=0)
    m1 = swap_tp(m0)

    q, pairs, normed1, gain_rows, w1, wo = call(
        qkv_kernel,
        [
            ((2, 2, 448, 128), BF),
            ((256, 128), BF),
            ((256, DP), BF),
            ((8, DP), F32),
            ((DP, 640), BF),
            ((DP, 512), BF),
        ],
        x, cosine, sine, *w1_pieces, name="qkv",
    )
    gain1 = gain_rows[0:1]
    gain2 = gain_rows[1:2]
    kv = ctx_gather(pairs)
    kv, w2_own = lax.optimization_barrier((kv, w2_own))
    w2 = jnp.concatenate(ctx_gather(w2_own), axis=0)
    att, lse = attn_fwd(block_order, own, zx, q, kv)
    att2 = att.reshape(256, 512)
    mixed = dotd(att2, wo, NT).reshape(2, 128, DP)
    h2 = xh + (pick(mixed, t) + swap_tp(pick(mixed, 1 - t).astype(BF)).astype(F32))
    unit2, scale2 = rms(h2)
    n0 = jnp.concatenate(fsdp_gather((unit2 * gain2).astype(BF)), axis=0)
    n1 = swap_tp(n0)
    first = mlp(n0, m0, w2)
    second = mlp(n1, m1, w2)

    dn2 = scatter_tokens(first[3], second[3])
    big = wgrads(n0, n1, m0, m1, first, second)
    big = total(ctx_scatter(row_blocks(big))).astype(BF).reshape(4, SLOT, 3 * FFB)

    back2, gg2 = rms_back(dn2, unit2, scale2, gain2)
    g2 = gh + back2
    dah = g2.astype(BF)
    da = both(dah, swap_tp(dah), t).reshape(256, DP)
    datt = dot(da, wo).astype(BF).reshape(2, 128, 512)
    dq, *dkv = attn_bwd(block_order, own, zx, q, kv, att, datt, lse)
    dkv = ctx_scatter(dkv)
    dproj, dn1 = call(
        dproj_kernel, [((256, 640), BF), ((256, DP), F32)], dq, cosine, sine, w1, *dkv, name="dproj"
    )
    dn1 = dn1.reshape(2, 128, DP)
    dn1h = pick(dn1, t) + swap_tp(pick(dn1, 1 - t).astype(BF)).astype(F32)
    unit1, scale1 = rms(xh)
    back1, gg1 = rms_back(dn1h, unit1, scale1, gain1)
    gin = unpad_features(g2 + back1, sel)
    grad_inputs = both(gin, swap_tp(gin), t)

    place = (jnp.arange(640)[None, :] == 576 + jnp.arange(2)[:, None]).astype(BF)
    gq = dotd(normed1, dproj, TN) + dotd(jnp.stack([gg1, gg2]).astype(BF), place, TN)
    gq = total(ctx_scatter(row_blocks(gq.astype(BF)))).astype(BF).reshape(4, SLOT, 640)
    gq = total(fsdp_exchange(gq, f))
    go = dotd(da, att2, TN).astype(BF)
    go = total(ctx_scatter(row_blocks(go))).astype(BF).reshape(4, SLOT, 512)
    go = total(fsdp_exchange(go, f))

    outh = unpad_features(h2 + scatter_tokens(first[4], second[4]), sel)
    outputs = both(outh, swap_tp(outh), t)

    hidden = fsdp_place(fsdp_exchange(big, f), f)[:, :ROWS].astype(F32).transpose(1, 0, 2)

    def columns(k):
        return hidden[:, :, k * FFB : k * FFB + FFB].reshape(ROWS, 4 * FFB)[:, :2432]

    grad_gate_up = jnp.stack([columns(0), columns(1)], axis=1)[None]
    grad_down = columns(2).T[None]
    grad_out = go[:ROWS, :448].T[None, None]
    grad_qkv = gq[None, :ROWS, None, :576]
    grad_bias = lax.dynamic_slice_in_dim(gq[ROWS, :576].reshape(9, HD), owner, 1, 1)[None, None]
    gg = gq[:ROWS, 576:578].T
    grad_gains = (gg + swap_tp(gg))[None]
    return (outputs, grad_inputs, grad_gains, grad_qkv, grad_bias, grad_out, grad_gate_up, grad_down)


def solution(mesh):
    in_specs = (
        P("fsdp", "ctx", None),
        P("fsdp", None),
        P("fsdp", "ctx", None),
        P(None, None, ("fsdp", "ctx")),
        P(None, ("fsdp", "ctx"), "tp", None),
        P(None, "tp", None, ("fsdp", "ctx")),
        P(None, "tp", None, ("fsdp", "ctx")),
        P(None, ("fsdp", "ctx"), None, "tp"),
        P(None, "tp", ("fsdp", "ctx")),
    )
    out_specs = (
        P("fsdp", "ctx", None),
        P("fsdp", "ctx", None),
        P(None, None, ("fsdp", "ctx")),
        P(None, ("fsdp", "ctx"), "tp", None),
        P(None, "tp", None, ("fsdp", "ctx")),
        P(None, "tp", None, ("fsdp", "ctx")),
        P(None, ("fsdp", "ctx"), None, "tp"),
        P(None, "tp", ("fsdp", "ctx")),
    )
    return jax.shard_map(body, mesh=mesh, in_specs=in_specs, out_specs=out_specs, check_vma=False)
```

```python
import math

import jax
import jax.numpy as jnp
from jax import lax
from jax.experimental import pallas as pl
from jax.experimental.pallas import tpu as pltpu
from jax.sharding import PartitionSpec as P

HD = 64
EPS = 1e-06
ROPE_BASE = 1000000.0
MASKED = -1e30
ROWS = 14
SLOT = 16
DM = 896
DP = 1024
OWNERS = 64
FFB = 640
CH = 256
GRP = ("ctx", "fsdp")
BF = jnp.bfloat16
F32 = jnp.float32
NT = (((1,), (1,)), ((), ()))
TN = (((0,), (0,)), ((), ()))
VMEM_ALL = pl.BlockSpec(memory_space=pltpu.VMEM)
PARAMS = pltpu.CompilerParams(vmem_limit_bytes=56 << 20)


def dot(a, b):
    return jnp.dot(a, b, preferred_element_type=F32)


def dotd(a, b, dims):
    return lax.dot_general(a, b, dims, preferred_element_type=F32)


def low(v):
    return lax.reduce_precision(v, 8, 7)


def selection():
    d = lax.broadcasted_iota(jnp.int32, (DM, DP), 0)
    p = lax.broadcasted_iota(jnp.int32, (DM, DP), 1)
    owner = d // ROWS
    return ((owner % 16) * 64 + (owner // 16) * SLOT + d % ROWS == p).astype(BF)


def split3(v):
    hi = low(v)
    rest = v - hi
    mid = low(rest)
    tail = rest - mid
    return jnp.concatenate([hi.astype(BF), mid.astype(BF), tail.astype(BF)], axis=0)


def sum3(v):
    n = v.shape[0] // 3
    return (v[:n] + v[n : 2 * n]) + v[2 * n :]


def pad_features(v, sel):
    return sum3(dot(split3(v), sel))


def unpad_features(v, sel):
    return sum3(dotd(split3(v), sel, NT))


def spread(v, count, axes):
    full = jnp.broadcast_to(v[None], (count,) + v.shape)
    return lax.all_to_all(full, axes, split_axis=0, concat_axis=0, tiled=True)


FSDP_STEPS = (0, 1, 3, 2)


def ring(v, k):
    return lax.ppermute(v, "fsdp", [(i, (i + k) % 4) for i in range(4)]) if k % 4 else v


def fsdp_gather(v):
    return [ring(v, k) for k in FSDP_STEPS]


def fsdp_place(parts, f):
    out = jnp.zeros((4,) + parts[0].shape, parts[0].dtype)
    for k, v in zip(FSDP_STEPS, parts):
        out = lax.dynamic_update_index_in_dim(out, v, (f - k) % 4, 0)
    return out


def fsdp_exchange(v, f):
    return [ring(pick(v, (f + k) % 4), k) for k in FSDP_STEPS]


def total(parts):
    out = parts[0].astype(F32)
    for v in parts[1:]:
        out = out + v.astype(F32)
    return out


def swap_tp(v):
    return lax.ppermute(v, "tp", [(0, 1), (1, 0)])


def lanes(shape):
    return lax.broadcasted_iota(jnp.int32, shape, len(shape) - 1)


def half_swap(v, lane):
    return jnp.where(lane % HD < HD // 2, pltpu.roll(v, 96, 1), pltpu.roll(v, 32, 1))


def qkv_kernel(x_ref, w_ref, cos_ref, sin_ref, q_ref, kv_ref, n_ref, g_ref):
    x = x_ref[...]
    scale = lax.rsqrt(jnp.sum(x * x, axis=-1, keepdims=True) * (1.0 / DM) + EPS)
    pick = (
        lax.broadcasted_iota(jnp.int32, (8, 128), 0) + HD
        == lax.broadcasted_iota(jnp.int32, (8, 128), 1)
    ) & (lax.broadcasted_iota(jnp.int32, (8, 128), 0) < 2)
    gain_rows = dotd(jnp.where(pick, 1.0, 0.0).astype(BF), w_ref[:, 512:640], NT)
    g_ref[...] = gain_rows
    wide = lanes(x.shape)
    normed = jnp.where(wide % SLOT == ROWS, 1.0, x * scale * gain_rows[0:1]).astype(BF)
    n_ref[...] = normed
    proj = dot(normed, w_ref[:, 0:640])
    cosine = cos_ref[...]
    sine = sin_ref[...]
    lane = lanes(cosine.shape)
    left = lane < HD
    rots = []
    for g in range(4):
        v = proj[:, g * 128 : g * 128 + 128]
        rots.append(v * cosine + half_swap(v, lane) * sine)
    for h in range(7):
        r = rots[h // 2]
        if h % 2:
            r = pltpu.roll(r, HD, 1)
        qh = jnp.where(left, r * 0.125, 0.0).astype(BF)
        for s in range(2):
            for b in range(2):
                q_ref[s, b, h * 64 : h * 64 + 64, :] = qh[s * 128 + b * 64 : s * 128 + b * 64 + 64]
    pair = jnp.where(
        left, pltpu.roll(rots[3], HD, 1), pltpu.roll(proj[:, 512:640], HD, 1)
    ).astype(BF)
    for c in range(kv_ref.shape[0]):
        kv_ref[c] = pair


def order_rows(bo_ref, s, kv_ref, kvs):
    for j in range(32):
        at = pl.multiple_of(bo_ref[s, j] * 64, 64)
        kvs[pl.ds(at, 64), :] = kv_ref[j // 2, 0, (j % 2) * 64 : (j % 2) * 64 + 64, :]


def allowed(block, j):
    key = j * CH + lax.broadcasted_iota(jnp.int32, (448, CH), 1)
    query = block * 64 + lax.broadcasted_iota(jnp.int32, (448, CH), 0) % 64
    return key <= query


def attn_fwd_kernel(bo_ref, own_ref, q_ref, kv_ref, att_ref, lse_ref, kvs, sbuf, mbuf, lbuf, obuf):
    s = pl.program_id(0)
    order_rows(bo_ref, s, kv_ref, kvs)
    for b in range(2):
        block = own_ref[s, b]
        count = block // 4 + 1
        q = q_ref[0, b]
        mbuf[...] = jnp.full(mbuf.shape, MASKED, F32)

        def first(j, carry):
            k = kvs[pl.ds(pl.multiple_of(j * CH, CH), CH), :]
            sc = jnp.where(allowed(block, j), dotd(q, k, NT), MASKED)
            sbuf[j] = sc
            mbuf[...] = jnp.maximum(mbuf[...], jnp.maximum(sc[:, :128], sc[:, 128:]))
            return carry

        lax.fori_loop(0, count, first, 0)
        top = jnp.max(mbuf[...], axis=-1, keepdims=True)
        lbuf[...] = jnp.zeros(lbuf.shape, F32)
        obuf[...] = jnp.zeros(obuf.shape, F32)

        def second(j, carry):
            k = kvs[pl.ds(pl.multiple_of(j * CH, CH), CH), :]
            p = jnp.exp(sbuf[j] - top)
            lbuf[...] += p[:, :128] + p[:, 128:]
            obuf[...] += dot(p.astype(BF), k)
            return carry

        lax.fori_loop(0, count, second, 0)
        total = jnp.sum(lbuf[...], axis=-1, keepdims=True)
        lse_ref[0, b] = jnp.broadcast_to(top + jnp.log(total), (448, 128))
        o = obuf[...] / total
        left = lanes((64, 128)) < HD
        for g in range(4):
            even = pltpu.roll(o[g * 128 : g * 128 + 64], HD, 1)
            odd = o[g * 128 + 64 : g * 128 + 128] if g < 3 else jnp.zeros((64, 128), F32)
            att_ref[0, b * 64 : b * 64 + 64, g * 128 : g * 128 + 128] = jnp.where(
                left, even, odd
            ).astype(BF)


def head_rows(ref, b):
    right = lanes((64, 128)) >= HD
    parts = []
    for h in range(7):
        g = h // 2
        v = ref[0, b * 64 : b * 64 + 64, g * 128 : g * 128 + 128].astype(F32)
        if h % 2 == 0:
            v = pltpu.roll(v, HD, 1)
        parts.append(jnp.where(right, v, 0.0))
    return jnp.concatenate(parts, axis=0)


def attn_bwd_kernel(
    bo_ref, own_ref, q_ref, kv_ref, att_ref, do_ref, lse_ref, dq_ref, dkv_ref, kvs, dkvs, dqb
):
    s = pl.program_id(0)
    order_rows(bo_ref, s, kv_ref, kvs)
    dkvs[...] = jnp.zeros(dkvs.shape, F32)
    for b in range(2):
        block = own_ref[s, b]
        count = block // 4 + 1
        q = q_ref[0, b]
        do32 = head_rows(do_ref, b)
        delta = jnp.sum(do32 * head_rows(att_ref, b), axis=-1, keepdims=True)
        do = do32.astype(BF)
        lse = lse_ref[0, b][:, 0:1]
        dqb[...] = jnp.zeros(dqb.shape, F32)

        def step(j, carry):
            at = pl.ds(pl.multiple_of(j * CH, CH), CH)
            k = kvs[at, :]
            p = jnp.where(allowed(block, j), jnp.exp(dotd(q, k, NT) - lse), 0.0)
            ds = (p * (dotd(do, k, NT) - delta)).astype(BF)
            dqb[...] += dot(ds, k)
            dkvs[at, :] += dotd(ds, q, TN) + dotd(p.astype(BF), do, TN)
            return carry

        lax.fori_loop(0, count, step, 0)
        dq_ref[0, b] = dqb[...] * 0.125
    for j in range(32):
        at = pl.multiple_of(bo_ref[s, j] * 64, 64)
        dkv_ref[j // 2, 0, (j % 2) * 64 : (j % 2) * 64 + 64, :] = dkvs[pl.ds(at, 64), :].astype(BF)


def dproj_kernel(dq_ref, dkv_ref, cos_ref, sin_ref, w_ref, dp_ref, dn_ref):
    dkv = dkv_ref[0].astype(F32)
    for c in range(1, dkv_ref.shape[0]):
        dkv = dkv + dkv_ref[c].astype(F32)
    cosine = cos_ref[...]
    sine = sin_ref[...]
    lane = lanes(cosine.shape)
    left = lane < HD

    def head(h):
        return jnp.concatenate(
            [dq_ref[s, b, h * 64 : h * 64 + 64, :] for s in range(2) for b in range(2)], axis=0
        )

    for g in range(4):
        odd = head(2 * g + 1) if g < 3 else dkv
        u = jnp.where(left, head(2 * g), pltpu.roll(odd, HD, 1))
        dp_ref[:, g * 128 : g * 128 + 128] = (u * cosine - half_swap(u, lane) * sine).astype(BF)
    dp_ref[:, 512:640] = jnp.where(left, pltpu.roll(dkv, HD, 1), 0.0).astype(BF)
    dn_ref[...] = dotd(dp_ref[...], w_ref[:, 0:640], NT)


def mlp_kernel(n_ref, dm_ref, w_ref, act_ref, dg_ref, du_ref, dn_ref, out_ref):
    n = n_ref[...]
    gate = dot(n, w_ref[:, 0:FFB])
    up = dot(n, w_ref[:, FFB : 2 * FFB])
    dact = dot(dm_ref[...], w_ref[:, 2 * FFB : 3 * FFB])
    sg = 1.0 / (1.0 + jnp.exp(-gate))
    silu = gate * sg
    act = (silu * up).astype(BF)
    dg = (dact * up * sg * (1.0 + gate * (1.0 - sg))).astype(BF)
    du = (dact * silu).astype(BF)
    act_ref[...] = act
    dg_ref[...] = dg
    du_ref[...] = du
    dn_ref[...] = (dotd(dg, w_ref[:, 0:FFB], NT) + dotd(du, w_ref[:, FFB : 2 * FFB], NT)).astype(BF)
    out_ref[...] = dotd(act, w_ref[:, 2 * FFB : 3 * FFB], NT).astype(BF)


def wgrad_kernel(
    n0, n1, m0, m1, a0, a1, g0, g1, u0, u1, out_ref
):
    out_ref[:, 0:FFB] = (dotd(n0[...], g0[...], TN) + dotd(n1[...], g1[...], TN)).astype(BF)
    out_ref[:, FFB : 2 * FFB] = (dotd(n0[...], u0[...], TN) + dotd(n1[...], u1[...], TN)).astype(BF)
    out_ref[:, 2 * FFB : 3 * FFB] = (
        dotd(m0[...], a0[...], TN) + dotd(m1[...], a1[...], TN)
    ).astype(BF)


def call(kernel, outs, *args, name=None):
    return pl.pallas_call(
        kernel,
        out_shape=[jax.ShapeDtypeStruct(s, t) for s, t in outs],
        in_specs=[VMEM_ALL] * len(args),
        out_specs=[VMEM_ALL] * len(outs),
        compiler_params=PARAMS,
        name=name,
    )(*args)


def attn_fwd(bo, own, q, kv):
    return pl.pallas_call(
        attn_fwd_kernel,
        out_shape=[
            jax.ShapeDtypeStruct((2, 128, 512), BF),
            jax.ShapeDtypeStruct((2, 2, 448, 128), F32),
        ],
        grid_spec=pltpu.PrefetchScalarGridSpec(
            num_scalar_prefetch=2,
            grid=(2,),
            in_specs=[
                pl.BlockSpec((1, 2, 448, 128), lambda s, *_: (s, 0, 0, 0)),
                pl.BlockSpec((16, 1, 128, 128), lambda s, *_: (0, s, 0, 0)),
            ],
            out_specs=[
                pl.BlockSpec((1, 128, 512), lambda s, *_: (s, 0, 0)),
                pl.BlockSpec((1, 2, 448, 128), lambda s, *_: (s, 0, 0, 0)),
            ],
            scratch_shapes=[
                pltpu.VMEM((2048, 128), BF),
                pltpu.VMEM((8, 448, CH), F32),
                pltpu.VMEM((448, 128), F32),
                pltpu.VMEM((448, 128), F32),
                pltpu.VMEM((448, 128), F32),
            ],
        ),
        compiler_params=PARAMS,
        name="attn_fwd",
    )(bo, own, q, kv)


def attn_bwd(bo, own, q, kv, att, datt, lse):
    per_seq = pl.BlockSpec((1, 2, 448, 128), lambda s, *_: (s, 0, 0, 0))
    tokens = pl.BlockSpec((1, 128, 512), lambda s, *_: (s, 0, 0))
    pairs = pl.BlockSpec((16, 1, 128, 128), lambda s, *_: (0, s, 0, 0))
    return pl.pallas_call(
        attn_bwd_kernel,
        out_shape=[
            jax.ShapeDtypeStruct((2, 2, 448, 128), F32),
            jax.ShapeDtypeStruct((16, 2, 128, 128), BF),
        ],
        grid_spec=pltpu.PrefetchScalarGridSpec(
            num_scalar_prefetch=2,
            grid=(2,),
            in_specs=[per_seq, pairs, tokens, tokens, per_seq],
            out_specs=[per_seq, pairs],
            scratch_shapes=[
                pltpu.VMEM((2048, 128), BF),
                pltpu.VMEM((2048, 128), F32),
                pltpu.VMEM((448, 128), F32),
            ],
        ),
        compiler_params=PARAMS,
        name="attn_bwd",
    )(bo, own, q, kv, att, datt, lse)


def mlp(n, dm, w2):
    tok = pl.BlockSpec((256, DP), lambda i: (i, 0))
    hid = pl.BlockSpec((256, FFB), lambda i: (i, 0))
    return pl.pallas_call(
        mlp_kernel,
        out_shape=[jax.ShapeDtypeStruct((512, FFB), BF)] * 3
        + [jax.ShapeDtypeStruct((512, DP), BF)] * 2,
        grid=(2,),
        in_specs=[
            tok,
            tok,
            pl.BlockSpec((DP, 3 * FFB), lambda i: (0, 0), pipeline_mode=pl.Buffered(1)),
        ],
        out_specs=[hid, hid, hid, tok, tok],
        compiler_params=PARAMS,
        name="mlp",
    )(n, dm, w2)


def wgrads(n0, n1, m0, m1, first, second):
    feat = pl.BlockSpec((512, 256), lambda i: (0, i))
    hid = pl.BlockSpec((512, FFB), lambda i: (0, 0))
    args = [n0, n1, m0, m1, first[0], second[0], first[1], second[1], first[2], second[2]]
    return pl.pallas_call(
        wgrad_kernel,
        out_shape=jax.ShapeDtypeStruct((DP, 3 * FFB), BF),
        grid=(4,),
        in_specs=[feat] * 4 + [hid] * 6,
        out_specs=pl.BlockSpec((256, 3 * FFB), lambda i: (i, 0)),
        compiler_params=PARAMS,
        name="wgrad",
    )(*args)


def rms(v):
    scale = lax.rsqrt(jnp.sum(v * v, axis=-1, keepdims=True) * (1.0 / DM) + EPS)
    return v * scale, scale


def rms_back(dn, unit, scale, gain):
    e = dn * gain
    mean = jnp.sum(e * unit, axis=-1, keepdims=True) * (1.0 / DM)
    return scale * (e - unit * mean), jnp.sum(dn * unit, axis=0)


def pick(v, index):
    return lax.dynamic_index_in_dim(v, index, 0, keepdims=False)


def both(own, other, t):
    return jnp.stack([jnp.where(t == 0, own, other), jnp.where(t == 0, other, own)])


def scatter_tokens(own, other):
    pair = (own.astype(F32) + swap_tp(other).astype(F32)).astype(BF).reshape(4, 128, DP)
    return total([ring(pair[i], -k) for i, k in enumerate(FSDP_STEPS)])


def body(inputs, block_order, cotangent, gains, w_qkv, b_qkv, w_out, w_gate_up, w_down):
    seqs, toks, width = inputs.shape
    ctx = lax.axis_index("ctx")
    t = lax.axis_index("tp")
    f = lax.axis_index("fsdp")
    owner = f * 16 + ctx
    sel = selection()

    bias_row = jnp.where(jnp.arange(HD) == owner, b_qkv[0, 0], jnp.zeros((), BF)).reshape(1, 9 * HD)
    patch1 = jnp.concatenate(
        [
            jnp.concatenate([w_qkv[0, :, 0, :], bias_row, jnp.zeros((1, 9 * HD), BF)], axis=0),
            jnp.pad(gains[0].T, ((0, 2), (0, HD - 2))),
            jnp.pad(w_out[0, 0].T, ((0, 2), (0, 64))),
        ],
        axis=1,
    )
    w1 = spread(patch1, OWNERS, GRP).reshape(DP, 1152)
    wo = w1[:, 640:]

    tall = jnp.pad(w_gate_up[0], ((0, 2), (0, 0), (0, 4 * FFB - 2432)))
    gate_parts = tall[:, 0].reshape(SLOT, 4, FFB).transpose(1, 0, 2)
    up_parts = tall[:, 1].reshape(SLOT, 4, FFB).transpose(1, 0, 2)
    down_parts = (
        jnp.pad(w_down[0].T, ((0, 2), (0, 4 * FFB - 2432)))
        .reshape(SLOT, 4, FFB)
        .transpose(1, 0, 2)
    )
    patch2 = jnp.concatenate([gate_parts, up_parts, down_parts], axis=2)
    w2_own = fsdp_place(fsdp_exchange(patch2, f), f).reshape(64, 3 * FFB)
    w2 = lax.all_gather(w2_own, "ctx", axis=0, tiled=True)

    own = lax.dynamic_slice_in_dim(block_order, 2 * ctx, 2, 1)
    pos = (own[:, :, None] * 64 + jnp.arange(64, dtype=jnp.int32)).reshape(seqs * toks, 1)
    lane = lax.broadcasted_iota(jnp.int32, (1, 128), 1)
    freq = jnp.exp((lane % 32).astype(F32) * (-2.0 * math.log(ROPE_BASE) / HD))
    angle = pos.astype(F32) * freq
    cosine = jnp.cos(angle)
    sine = jnp.where(lane % HD < HD // 2, -1.0, 1.0) * jnp.sin(angle)

    x = pad_features(inputs.reshape(seqs * toks, width), sel)
    g = pad_features(cotangent.reshape(seqs * toks, width), sel)
    xh = pick(x.reshape(2, 128, DP), t)
    gh = pick(g.reshape(2, 128, DP), t)
    m0 = jnp.concatenate(fsdp_gather(gh.astype(BF)), axis=0)
    m1 = swap_tp(m0)

    q, pairs, normed1, gain_rows = call(
        qkv_kernel,
        [((2, 2, 448, 128), BF), ((16, 256, 128), BF), ((256, DP), BF), ((8, DP), F32)],
        x, w1, cosine, sine, name="qkv",
    )
    gain1 = gain_rows[0:1]
    gain2 = gain_rows[1:2]
    kv = lax.all_to_all(pairs, "ctx", split_axis=0, concat_axis=0, tiled=True).reshape(
        16, 2, 128, 128
    )
    att, lse = attn_fwd(block_order, own, q, kv)
    att2 = att.reshape(256, 512)
    mixed = dotd(att2, wo, NT).reshape(2, 128, DP)
    h2 = xh + (pick(mixed, t) + swap_tp(pick(mixed, 1 - t).astype(BF)).astype(F32))
    unit2, scale2 = rms(h2)
    n0 = jnp.concatenate(fsdp_gather((unit2 * gain2).astype(BF)), axis=0)
    n1 = swap_tp(n0)
    first = mlp(n0, m0, w2)
    second = mlp(n1, m1, w2)

    dn2 = scatter_tokens(first[3], second[3])
    big = wgrads(n0, n1, m0, m1, first, second).reshape(OWNERS, SLOT, 3 * FFB)
    big = lax.all_to_all(big, GRP, split_axis=0, concat_axis=0, tiled=True)

    back2, gg2 = rms_back(dn2, unit2, scale2, gain2)
    g2 = gh + back2
    dah = g2.astype(BF)
    da = both(dah, swap_tp(dah), t).reshape(256, DP)
    datt = dot(da, wo).astype(BF).reshape(2, 128, 512)
    dq, dkv = attn_bwd(block_order, own, q, kv, att, datt, lse)
    dkv, big = lax.optimization_barrier((dkv, big))
    dkv = lax.all_to_all(dkv, "ctx", split_axis=0, concat_axis=0, tiled=True).reshape(16, 256, 128)
    dproj, dn1 = call(
        dproj_kernel, [((256, 640), BF), ((256, DP), F32)], dq, dkv, cosine, sine, w1, name="dproj"
    )
    dn1 = dn1.reshape(2, 128, DP)
    dn1h = pick(dn1, t) + swap_tp(pick(dn1, 1 - t).astype(BF)).astype(F32)
    unit1, scale1 = rms(xh)
    back1, gg1 = rms_back(dn1h, unit1, scale1, gain1)
    gin = unpad_features(g2 + back1, sel)
    grad_inputs = both(gin, swap_tp(gin), t)

    place = (jnp.arange(640)[None, :] == 576 + jnp.arange(2)[:, None]).astype(BF)
    gq = dotd(normed1, dproj, TN) + dotd(jnp.stack([gg1, gg2]).astype(BF), place, TN)
    last = jnp.concatenate([gq.astype(BF), dotd(da, att2, TN).astype(BF)], axis=1)
    last = lax.all_to_all(
        last.reshape(OWNERS, SLOT, 1152), GRP, split_axis=0, concat_axis=0, tiled=True
    )

    outh = h2 + scatter_tokens(first[4], second[4])
    outh = unpad_features(outh, sel)
    outputs = both(outh, swap_tp(outh), t)

    big = jnp.sum(big.reshape(16, 4, SLOT, 3 * FFB).astype(F32), axis=0)
    hidden = big[:, :ROWS, : 3 * FFB].transpose(1, 0, 2)

    def columns(k):
        return hidden[:, :, k * FFB : k * FFB + FFB].reshape(ROWS, 4 * FFB)[:, :2432]

    grad_gate_up = jnp.stack([columns(0), columns(1)], axis=1)[None]
    grad_down = columns(2).T[None]
    gq = jnp.sum(last.astype(F32), axis=0)
    grad_out = gq[:ROWS, 640:1088].T[None, None]
    grad_qkv = gq[None, :ROWS, None, :576]
    grad_bias = lax.dynamic_slice_in_dim(gq[ROWS, :576].reshape(9, HD), owner, 1, 1)[None, None]
    gg = gq[:ROWS, 576:578].T
    grad_gains = (gg + swap_tp(gg))[None]
    return (outputs, grad_inputs, grad_gains, grad_qkv, grad_bias, grad_out, grad_gate_up, grad_down)


def solution(mesh):
    in_specs = (
        P("fsdp", "ctx", None),
        P("fsdp", None),
        P("fsdp", "ctx", None),
        P(None, None, ("fsdp", "ctx")),
        P(None, ("fsdp", "ctx"), "tp", None),
        P(None, "tp", None, ("fsdp", "ctx")),
        P(None, "tp", None, ("fsdp", "ctx")),
        P(None, ("fsdp", "ctx"), None, "tp"),
        P(None, "tp", ("fsdp", "ctx")),
    )
    out_specs = (
        P("fsdp", "ctx", None),
        P("fsdp", "ctx", None),
        P(None, None, ("fsdp", "ctx")),
        P(None, ("fsdp", "ctx"), "tp", None),
        P(None, "tp", None, ("fsdp", "ctx")),
        P(None, "tp", None, ("fsdp", "ctx")),
        P(None, ("fsdp", "ctx"), None, "tp"),
        P(None, "tp", ("fsdp", "ctx")),
    )
    return jax.shard_map(body, mesh=mesh, in_specs=in_specs, out_specs=out_specs, check_vma=False)
```

```python
import math

import jax
import jax.numpy as jnp
from jax import lax
from jax.experimental import pallas as pl
from jax.experimental.pallas import tpu as pltpu
from jax.sharding import PartitionSpec as P

HD = 64
EPS = 1e-06
ROPE_BASE = 1000000.0
MASKED = -1e30
ROWS = 14
SLOT = 16
DM = 896
DP = 1024
OWNERS = 64
FFB = 640
CH = 256
GRP = ("ctx", "fsdp")
BF = jnp.bfloat16
F32 = jnp.float32
NT = (((1,), (1,)), ((), ()))
TN = (((0,), (0,)), ((), ()))
VMEM_ALL = pl.BlockSpec(memory_space=pltpu.VMEM)
PARAMS = pltpu.CompilerParams(vmem_limit_bytes=56 << 20)


def dot(a, b):
    return jnp.dot(a, b, preferred_element_type=F32)


def dotd(a, b, dims):
    return lax.dot_general(a, b, dims, preferred_element_type=F32)


def low(v):
    return lax.reduce_precision(v, 8, 7)


def selection():
    d = lax.broadcasted_iota(jnp.int32, (DM, DP), 0)
    p = lax.broadcasted_iota(jnp.int32, (DM, DP), 1)
    owner = d // ROWS
    return ((owner % 16) * 64 + (owner // 16) * SLOT + d % ROWS == p).astype(BF)


def split3(v):
    hi = low(v)
    rest = v - hi
    mid = low(rest)
    tail = rest - mid
    return jnp.concatenate([hi.astype(BF), mid.astype(BF), tail.astype(BF)], axis=0)


def sum3(v):
    n = v.shape[0] // 3
    return (v[:n] + v[n : 2 * n]) + v[2 * n :]


def pad_features(v, sel):
    return sum3(dot(split3(v), sel))


def unpad_features(v, sel):
    return sum3(dotd(split3(v), sel, NT))


def spread(v, count, axes):
    full = jnp.broadcast_to(v[None], (count,) + v.shape)
    return lax.all_to_all(full, axes, split_axis=0, concat_axis=0, tiled=True)


FSDP_STEPS = (0, 1, 3, 2)


def ring(v, k):
    return lax.ppermute(v, "fsdp", [(i, (i + k) % 4) for i in range(4)]) if k % 4 else v


def fsdp_gather(v):
    return [ring(v, k) for k in FSDP_STEPS]


def fsdp_place(parts, f):
    out = jnp.zeros((4,) + parts[0].shape, parts[0].dtype)
    for k, v in zip(FSDP_STEPS, parts):
        out = lax.dynamic_update_index_in_dim(out, v, (f - k) % 4, 0)
    return out


def fsdp_exchange(v, f):
    return [ring(pick(v, (f + k) % 4), k) for k in FSDP_STEPS]


def total(parts):
    out = parts[0].astype(F32)
    for v in parts[1:]:
        out = out + v.astype(F32)
    return out


def swap_tp(v):
    return lax.ppermute(v, "tp", [(0, 1), (1, 0)])


def lanes(shape):
    return lax.broadcasted_iota(jnp.int32, shape, len(shape) - 1)


def half_swap(v, lane):
    return jnp.where(lane % HD < HD // 2, pltpu.roll(v, 96, 1), pltpu.roll(v, 32, 1))


def qkv_kernel(x_ref, w_ref, cos_ref, sin_ref, q_ref, kv_ref, n_ref, g_ref):
    x = x_ref[...]
    scale = lax.rsqrt(jnp.sum(x * x, axis=-1, keepdims=True) * (1.0 / DM) + EPS)
    pick = (
        lax.broadcasted_iota(jnp.int32, (8, 128), 0) + HD
        == lax.broadcasted_iota(jnp.int32, (8, 128), 1)
    ) & (lax.broadcasted_iota(jnp.int32, (8, 128), 0) < 2)
    gain_rows = dotd(jnp.where(pick, 1.0, 0.0).astype(BF), w_ref[:, 512:640], NT)
    g_ref[...] = gain_rows
    wide = lanes(x.shape)
    normed = jnp.where(wide % SLOT == ROWS, 1.0, x * scale * gain_rows[0:1]).astype(BF)
    n_ref[...] = normed
    proj = dot(normed, w_ref[:, 0:640])
    cosine = cos_ref[...]
    sine = sin_ref[...]
    lane = lanes(cosine.shape)
    left = lane < HD
    rots = []
    for g in range(4):
        v = proj[:, g * 128 : g * 128 + 128]
        rots.append(v * cosine + half_swap(v, lane) * sine)
    for h in range(7):
        r = rots[h // 2]
        if h % 2:
            r = pltpu.roll(r, HD, 1)
        qh = jnp.where(left, r * 0.125, 0.0).astype(BF)
        for s in range(2):
            for b in range(2):
                q_ref[s, b, h * 64 : h * 64 + 64, :] = qh[s * 128 + b * 64 : s * 128 + b * 64 + 64]
    pair = jnp.where(
        left, pltpu.roll(rots[3], HD, 1), pltpu.roll(proj[:, 512:640], HD, 1)
    ).astype(BF)
    for c in range(kv_ref.shape[0]):
        kv_ref[c] = pair


def order_rows(bo_ref, s, kv_ref, kvs):
    for j in range(32):
        at = pl.multiple_of(bo_ref[s, j] * 64, 64)
        kvs[pl.ds(at, 64), :] = kv_ref[j // 2, 0, (j % 2) * 64 : (j % 2) * 64 + 64, :]


def allowed(block, j):
    key = j * CH + lax.broadcasted_iota(jnp.int32, (448, CH), 1)
    query = block * 64 + lax.broadcasted_iota(jnp.int32, (448, CH), 0) % 64
    return key <= query


def attn_fwd_kernel(bo_ref, own_ref, q_ref, kv_ref, att_ref, lse_ref, kvs, sbuf, mbuf, lbuf, obuf):
    s = pl.program_id(0)
    order_rows(bo_ref, s, kv_ref, kvs)
    for b in range(2):
        block = own_ref[s, b]
        count = block // 4 + 1
        q = q_ref[0, b]
        mbuf[...] = jnp.full(mbuf.shape, MASKED, F32)

        def first(j, carry):
            k = kvs[pl.ds(pl.multiple_of(j * CH, CH), CH), :]
            sc = jnp.where(allowed(block, j), dotd(q, k, NT), MASKED)
            sbuf[j] = sc
            mbuf[...] = jnp.maximum(mbuf[...], jnp.maximum(sc[:, :128], sc[:, 128:]))
            return carry

        lax.fori_loop(0, count, first, 0)
        top = jnp.max(mbuf[...], axis=-1, keepdims=True)
        lbuf[...] = jnp.zeros(lbuf.shape, F32)
        obuf[...] = jnp.zeros(obuf.shape, F32)

        def second(j, carry):
            k = kvs[pl.ds(pl.multiple_of(j * CH, CH), CH), :]
            p = jnp.exp(sbuf[j] - top)
            lbuf[...] += p[:, :128] + p[:, 128:]
            obuf[...] += dot(p.astype(BF), k)
            return carry

        lax.fori_loop(0, count, second, 0)
        total = jnp.sum(lbuf[...], axis=-1, keepdims=True)
        lse_ref[0, b] = jnp.broadcast_to(top + jnp.log(total), (448, 128))
        o = obuf[...] / total
        left = lanes((64, 128)) < HD
        for g in range(4):
            even = pltpu.roll(o[g * 128 : g * 128 + 64], HD, 1)
            odd = o[g * 128 + 64 : g * 128 + 128] if g < 3 else jnp.zeros((64, 128), F32)
            att_ref[0, b * 64 : b * 64 + 64, g * 128 : g * 128 + 128] = jnp.where(
                left, even, odd
            ).astype(BF)


def head_rows(ref, b):
    right = lanes((64, 128)) >= HD
    parts = []
    for h in range(7):
        g = h // 2
        v = ref[0, b * 64 : b * 64 + 64, g * 128 : g * 128 + 128].astype(F32)
        if h % 2 == 0:
            v = pltpu.roll(v, HD, 1)
        parts.append(jnp.where(right, v, 0.0))
    return jnp.concatenate(parts, axis=0)


def attn_bwd_kernel(
    bo_ref, own_ref, q_ref, kv_ref, att_ref, do_ref, lse_ref, dq_ref, dkv_ref, kvs, dkvs, dqb
):
    s = pl.program_id(0)
    order_rows(bo_ref, s, kv_ref, kvs)
    dkvs[...] = jnp.zeros(dkvs.shape, F32)
    for b in range(2):
        block = own_ref[s, b]
        count = block // 4 + 1
        q = q_ref[0, b]
        do32 = head_rows(do_ref, b)
        delta = jnp.sum(do32 * head_rows(att_ref, b), axis=-1, keepdims=True)
        do = do32.astype(BF)
        lse = lse_ref[0, b][:, 0:1]
        dqb[...] = jnp.zeros(dqb.shape, F32)

        def step(j, carry):
            at = pl.ds(pl.multiple_of(j * CH, CH), CH)
            k = kvs[at, :]
            p = jnp.where(allowed(block, j), jnp.exp(dotd(q, k, NT) - lse), 0.0)
            ds = (p * (dotd(do, k, NT) - delta)).astype(BF)
            dqb[...] += dot(ds, k)
            dkvs[at, :] += dotd(ds, q, TN) + dotd(p.astype(BF), do, TN)
            return carry

        lax.fori_loop(0, count, step, 0)
        dq_ref[0, b] = dqb[...] * 0.125
    for j in range(32):
        at = pl.multiple_of(bo_ref[s, j] * 64, 64)
        dkv_ref[j // 2, 0, (j % 2) * 64 : (j % 2) * 64 + 64, :] = dkvs[pl.ds(at, 64), :].astype(BF)


def dproj_kernel(dq_ref, dkv_ref, cos_ref, sin_ref, w_ref, dp_ref, dn_ref):
    dkv = dkv_ref[0].astype(F32)
    for c in range(1, dkv_ref.shape[0]):
        dkv = dkv + dkv_ref[c].astype(F32)
    cosine = cos_ref[...]
    sine = sin_ref[...]
    lane = lanes(cosine.shape)
    left = lane < HD

    def head(h):
        return jnp.concatenate(
            [dq_ref[s, b, h * 64 : h * 64 + 64, :] for s in range(2) for b in range(2)], axis=0
        )

    for g in range(4):
        odd = head(2 * g + 1) if g < 3 else dkv
        u = jnp.where(left, head(2 * g), pltpu.roll(odd, HD, 1))
        dp_ref[:, g * 128 : g * 128 + 128] = (u * cosine - half_swap(u, lane) * sine).astype(BF)
    dp_ref[:, 512:640] = jnp.where(left, pltpu.roll(dkv, HD, 1), 0.0).astype(BF)
    dn_ref[...] = dotd(dp_ref[...], w_ref[:, 0:640], NT)


def mlp_kernel(n_ref, dm_ref, w_ref, act_ref, dg_ref, du_ref, dn_ref, out_ref):
    n = n_ref[...]
    gate = dot(n, w_ref[:, 0:FFB])
    up = dot(n, w_ref[:, FFB : 2 * FFB])
    dact = dot(dm_ref[...], w_ref[:, 2 * FFB : 3 * FFB])
    sg = 1.0 / (1.0 + jnp.exp(-gate))
    silu = gate * sg
    act = (silu * up).astype(BF)
    dg = (dact * up * sg * (1.0 + gate * (1.0 - sg))).astype(BF)
    du = (dact * silu).astype(BF)
    act_ref[...] = act
    dg_ref[...] = dg
    du_ref[...] = du
    dn_ref[...] = (dotd(dg, w_ref[:, 0:FFB], NT) + dotd(du, w_ref[:, FFB : 2 * FFB], NT)).astype(BF)
    out_ref[...] = dotd(act, w_ref[:, 2 * FFB : 3 * FFB], NT).astype(BF)


def wgrad_kernel(
    n0, n1, m0, m1, a0, a1, g0, g1, u0, u1, out_ref
):
    out_ref[:, 0:FFB] = (dotd(n0[...], g0[...], TN) + dotd(n1[...], g1[...], TN)).astype(BF)
    out_ref[:, FFB : 2 * FFB] = (dotd(n0[...], u0[...], TN) + dotd(n1[...], u1[...], TN)).astype(BF)
    out_ref[:, 2 * FFB : 3 * FFB] = (
        dotd(m0[...], a0[...], TN) + dotd(m1[...], a1[...], TN)
    ).astype(BF)


def call(kernel, outs, *args, name=None):
    return pl.pallas_call(
        kernel,
        out_shape=[jax.ShapeDtypeStruct(s, t) for s, t in outs],
        in_specs=[VMEM_ALL] * len(args),
        out_specs=[VMEM_ALL] * len(outs),
        compiler_params=PARAMS,
        name=name,
    )(*args)


def attn_fwd(bo, own, q, kv):
    return pl.pallas_call(
        attn_fwd_kernel,
        out_shape=[
            jax.ShapeDtypeStruct((2, 128, 512), BF),
            jax.ShapeDtypeStruct((2, 2, 448, 128), F32),
        ],
        grid_spec=pltpu.PrefetchScalarGridSpec(
            num_scalar_prefetch=2,
            grid=(2,),
            in_specs=[
                pl.BlockSpec((1, 2, 448, 128), lambda s, *_: (s, 0, 0, 0)),
                pl.BlockSpec((16, 1, 128, 128), lambda s, *_: (0, s, 0, 0)),
            ],
            out_specs=[
                pl.BlockSpec((1, 128, 512), lambda s, *_: (s, 0, 0)),
                pl.BlockSpec((1, 2, 448, 128), lambda s, *_: (s, 0, 0, 0)),
            ],
            scratch_shapes=[
                pltpu.VMEM((2048, 128), BF),
                pltpu.VMEM((8, 448, CH), F32),
                pltpu.VMEM((448, 128), F32),
                pltpu.VMEM((448, 128), F32),
                pltpu.VMEM((448, 128), F32),
            ],
        ),
        compiler_params=PARAMS,
        name="attn_fwd",
    )(bo, own, q, kv)


def attn_bwd(bo, own, q, kv, att, datt, lse):
    per_seq = pl.BlockSpec((1, 2, 448, 128), lambda s, *_: (s, 0, 0, 0))
    tokens = pl.BlockSpec((1, 128, 512), lambda s, *_: (s, 0, 0))
    pairs = pl.BlockSpec((16, 1, 128, 128), lambda s, *_: (0, s, 0, 0))
    return pl.pallas_call(
        attn_bwd_kernel,
        out_shape=[
            jax.ShapeDtypeStruct((2, 2, 448, 128), F32),
            jax.ShapeDtypeStruct((16, 2, 128, 128), BF),
        ],
        grid_spec=pltpu.PrefetchScalarGridSpec(
            num_scalar_prefetch=2,
            grid=(2,),
            in_specs=[per_seq, pairs, tokens, tokens, per_seq],
            out_specs=[per_seq, pairs],
            scratch_shapes=[
                pltpu.VMEM((2048, 128), BF),
                pltpu.VMEM((2048, 128), F32),
                pltpu.VMEM((448, 128), F32),
            ],
        ),
        compiler_params=PARAMS,
        name="attn_bwd",
    )(bo, own, q, kv, att, datt, lse)


def mlp(n, dm, w2):
    tok = pl.BlockSpec((256, DP), lambda i: (i, 0))
    hid = pl.BlockSpec((256, FFB), lambda i: (i, 0))
    return pl.pallas_call(
        mlp_kernel,
        out_shape=[jax.ShapeDtypeStruct((512, FFB), BF)] * 3
        + [jax.ShapeDtypeStruct((512, DP), BF)] * 2,
        grid=(2,),
        in_specs=[
            tok,
            tok,
            pl.BlockSpec((DP, 3 * FFB), lambda i: (0, 0), pipeline_mode=pl.Buffered(1)),
        ],
        out_specs=[hid, hid, hid, tok, tok],
        compiler_params=PARAMS,
        name="mlp",
    )(n, dm, w2)


def wgrads(n0, n1, m0, m1, first, second):
    feat = pl.BlockSpec((512, 256), lambda i: (0, i))
    hid = pl.BlockSpec((512, FFB), lambda i: (0, 0))
    args = [n0, n1, m0, m1, first[0], second[0], first[1], second[1], first[2], second[2]]
    return pl.pallas_call(
        wgrad_kernel,
        out_shape=jax.ShapeDtypeStruct((DP, 3 * FFB), BF),
        grid=(4,),
        in_specs=[feat] * 4 + [hid] * 6,
        out_specs=pl.BlockSpec((256, 3 * FFB), lambda i: (i, 0)),
        compiler_params=PARAMS,
        name="wgrad",
    )(*args)


def rms(v):
    scale = lax.rsqrt(jnp.sum(v * v, axis=-1, keepdims=True) * (1.0 / DM) + EPS)
    return v * scale, scale


def rms_back(dn, unit, scale, gain):
    e = dn * gain
    mean = jnp.sum(e * unit, axis=-1, keepdims=True) * (1.0 / DM)
    return scale * (e - unit * mean), jnp.sum(dn * unit, axis=0)


def pick(v, index):
    return lax.dynamic_index_in_dim(v, index, 0, keepdims=False)


def both(own, other, t):
    return jnp.stack([jnp.where(t == 0, own, other), jnp.where(t == 0, other, own)])


def tp_sum(own, other):
    return (own.astype(F32) + swap_tp(other).astype(F32)).astype(BF).reshape(4, 128, DP)


def fsdp_scatter(pair):
    return total([ring(pair[i], -k) for i, k in enumerate(FSDP_STEPS)])


def body(inputs, block_order, cotangent, gains, w_qkv, b_qkv, w_out, w_gate_up, w_down):
    seqs, toks, width = inputs.shape
    ctx = lax.axis_index("ctx")
    t = lax.axis_index("tp")
    f = lax.axis_index("fsdp")
    owner = f * 16 + ctx
    sel = selection()

    bias_row = jnp.where(jnp.arange(HD) == owner, b_qkv[0, 0], jnp.zeros((), BF)).reshape(1, 9 * HD)
    patch1 = jnp.concatenate(
        [
            jnp.concatenate([w_qkv[0, :, 0, :], bias_row, jnp.zeros((1, 9 * HD), BF)], axis=0),
            jnp.pad(gains[0].T, ((0, 2), (0, HD - 2))),
            jnp.pad(w_out[0, 0].T, ((0, 2), (0, 64))),
        ],
        axis=1,
    )
    w1 = spread(patch1, OWNERS, GRP).reshape(DP, 1152)
    wo = w1[:, 640:]

    tall = jnp.pad(w_gate_up[0], ((0, 2), (0, 0), (0, 4 * FFB - 2432)))
    gate_parts = tall[:, 0].reshape(SLOT, 4, FFB).transpose(1, 0, 2)
    up_parts = tall[:, 1].reshape(SLOT, 4, FFB).transpose(1, 0, 2)
    down_parts = (
        jnp.pad(w_down[0].T, ((0, 2), (0, 4 * FFB - 2432)))
        .reshape(SLOT, 4, FFB)
        .transpose(1, 0, 2)
    )
    patch2 = jnp.concatenate([gate_parts, up_parts, down_parts], axis=2)
    w2_own = fsdp_place(fsdp_exchange(patch2, f), f).reshape(64, 3 * FFB)
    w2 = lax.all_gather(w2_own, "ctx", axis=0, tiled=True)

    own = lax.dynamic_slice_in_dim(block_order, 2 * ctx, 2, 1)
    pos = (own[:, :, None] * 64 + jnp.arange(64, dtype=jnp.int32)).reshape(seqs * toks, 1)
    lane = lax.broadcasted_iota(jnp.int32, (1, 128), 1)
    freq = jnp.exp((lane % 32).astype(F32) * (-2.0 * math.log(ROPE_BASE) / HD))
    angle = pos.astype(F32) * freq
    cosine = jnp.cos(angle)
    sine = jnp.where(lane % HD < HD // 2, -1.0, 1.0) * jnp.sin(angle)

    x = pad_features(inputs.reshape(seqs * toks, width), sel)
    g = pad_features(cotangent.reshape(seqs * toks, width), sel)
    xh = pick(x.reshape(2, 128, DP), t)
    gh = pick(g.reshape(2, 128, DP), t)
    m0 = jnp.concatenate(fsdp_gather(gh.astype(BF)), axis=0)
    m1 = swap_tp(m0)

    q, pairs, normed1, gain_rows = call(
        qkv_kernel,
        [((2, 2, 448, 128), BF), ((16, 256, 128), BF), ((256, DP), BF), ((8, DP), F32)],
        x, w1, cosine, sine, name="qkv",
    )
    gain1 = gain_rows[0:1]
    gain2 = gain_rows[1:2]
    kv = lax.all_to_all(pairs, "ctx", split_axis=0, concat_axis=0, tiled=True).reshape(
        16, 2, 128, 128
    )
    att, lse = attn_fwd(block_order, own, q, kv)
    att2 = att.reshape(256, 512)
    mixed = dotd(att2, wo, NT).reshape(2, 128, DP)
    h2 = xh + (pick(mixed, t) + swap_tp(pick(mixed, 1 - t).astype(BF)).astype(F32))
    unit2, scale2 = rms(h2)
    n0 = jnp.concatenate(fsdp_gather((unit2 * gain2).astype(BF)), axis=0)
    n1 = swap_tp(n0)
    first = mlp(n0, m0, w2)
    second = mlp(n1, m1, w2)

    dn2 = fsdp_scatter(tp_sum(first[3], second[3]))
    out_pair = tp_sum(first[4], second[4])
    big = wgrads(n0, n1, m0, m1, first, second).reshape(OWNERS, SLOT, 3 * FFB)
    big, _ = lax.optimization_barrier((big, dn2))
    big = lax.all_to_all(big, GRP, split_axis=0, concat_axis=0, tiled=True)

    back2, gg2 = rms_back(dn2, unit2, scale2, gain2)
    g2 = gh + back2
    dah = g2.astype(BF)
    da = both(dah, swap_tp(dah), t).reshape(256, DP)
    datt = dot(da, wo).astype(BF).reshape(2, 128, 512)
    dq, dkv = attn_bwd(block_order, own, q, kv, att, datt, lse)
    dkv, big = lax.optimization_barrier((dkv, big))
    dkv = lax.all_to_all(dkv, "ctx", split_axis=0, concat_axis=0, tiled=True).reshape(16, 256, 128)
    out_pair, _ = lax.optimization_barrier((out_pair, dkv))
    dproj, dn1 = call(
        dproj_kernel, [((256, 640), BF), ((256, DP), F32)], dq, dkv, cosine, sine, w1, name="dproj"
    )
    dn1 = dn1.reshape(2, 128, DP)
    dn1h = pick(dn1, t) + swap_tp(pick(dn1, 1 - t).astype(BF)).astype(F32)
    unit1, scale1 = rms(xh)
    back1, gg1 = rms_back(dn1h, unit1, scale1, gain1)
    gin = unpad_features(g2 + back1, sel)
    grad_inputs = both(gin, swap_tp(gin), t)

    place = (jnp.arange(640)[None, :] == 576 + jnp.arange(2)[:, None]).astype(BF)
    gq = dotd(normed1, dproj, TN) + dotd(jnp.stack([gg1, gg2]).astype(BF), place, TN)
    last = jnp.concatenate([gq.astype(BF), dotd(da, att2, TN).astype(BF)], axis=1)
    last = lax.all_to_all(
        last.reshape(OWNERS, SLOT, 1152), GRP, split_axis=0, concat_axis=0, tiled=True
    )

    outh = h2 + fsdp_scatter(out_pair)
    outh = unpad_features(outh, sel)
    outputs = both(outh, swap_tp(outh), t)

    big = jnp.sum(big.reshape(16, 4, SLOT, 3 * FFB).astype(F32), axis=0)
    hidden = big[:, :ROWS, : 3 * FFB].transpose(1, 0, 2)

    def columns(k):
        return hidden[:, :, k * FFB : k * FFB + FFB].reshape(ROWS, 4 * FFB)[:, :2432]

    grad_gate_up = jnp.stack([columns(0), columns(1)], axis=1)[None]
    grad_down = columns(2).T[None]
    gq = jnp.sum(last.astype(F32), axis=0)
    grad_out = gq[:ROWS, 640:1088].T[None, None]
    grad_qkv = gq[None, :ROWS, None, :576]
    grad_bias = lax.dynamic_slice_in_dim(gq[ROWS, :576].reshape(9, HD), owner, 1, 1)[None, None]
    gg = gq[:ROWS, 576:578].T
    grad_gains = (gg + swap_tp(gg))[None]
    return (outputs, grad_inputs, grad_gains, grad_qkv, grad_bias, grad_out, grad_gate_up, grad_down)


def solution(mesh):
    in_specs = (
        P("fsdp", "ctx", None),
        P("fsdp", None),
        P("fsdp", "ctx", None),
        P(None, None, ("fsdp", "ctx")),
        P(None, ("fsdp", "ctx"), "tp", None),
        P(None, "tp", None, ("fsdp", "ctx")),
        P(None, "tp", None, ("fsdp", "ctx")),
        P(None, ("fsdp", "ctx"), None, "tp"),
        P(None, "tp", ("fsdp", "ctx")),
    )
    out_specs = (
        P("fsdp", "ctx", None),
        P("fsdp", "ctx", None),
        P(None, None, ("fsdp", "ctx")),
        P(None, ("fsdp", "ctx"), "tp", None),
        P(None, "tp", None, ("fsdp", "ctx")),
        P(None, "tp", None, ("fsdp", "ctx")),
        P(None, ("fsdp", "ctx"), None, "tp"),
        P(None, "tp", ("fsdp", "ctx")),
    )
    return jax.shard_map(body, mesh=mesh, in_specs=in_specs, out_specs=out_specs, check_vma=False)
```

```python
import math

import jax
import jax.numpy as jnp
from jax import lax
from jax.experimental import pallas as pl
from jax.experimental.pallas import tpu as pltpu
from jax.sharding import PartitionSpec as P

HD = 64
EPS = 1e-06
ROPE_BASE = 1000000.0
MASKED = -1e30
ROWS = 14
SLOT = 16
DM = 896
DP = 1024
OWNERS = 64
FFB = 640
CH = 256
GRP = ("ctx", "fsdp")
BF = jnp.bfloat16
F32 = jnp.float32
NT = (((1,), (1,)), ((), ()))
TN = (((0,), (0,)), ((), ()))
VMEM_ALL = pl.BlockSpec(memory_space=pltpu.VMEM)
PARAMS = pltpu.CompilerParams(vmem_limit_bytes=56 << 20)


def dot(a, b):
    return jnp.dot(a, b, preferred_element_type=F32)


def dotd(a, b, dims):
    return lax.dot_general(a, b, dims, preferred_element_type=F32)


def low(v):
    return lax.reduce_precision(v, 8, 7)


def selection():
    d = lax.broadcasted_iota(jnp.int32, (DM, DP), 0)
    p = lax.broadcasted_iota(jnp.int32, (DM, DP), 1)
    owner = d // ROWS
    return ((owner % 16) * 64 + (owner // 16) * SLOT + d % ROWS == p).astype(BF)


def split3(v):
    hi = low(v)
    rest = v - hi
    mid = low(rest)
    tail = rest - mid
    return jnp.concatenate([hi.astype(BF), mid.astype(BF), tail.astype(BF)], axis=0)


def sum3(v):
    n = v.shape[0] // 3
    return (v[:n] + v[n : 2 * n]) + v[2 * n :]


def pad_features(v, sel):
    return sum3(dot(split3(v), sel))


def unpad_features(v, sel):
    return sum3(dotd(split3(v), sel, NT))


def spread(v, count, axes):
    full = jnp.broadcast_to(v[None], (count,) + v.shape)
    return lax.all_to_all(full, axes, split_axis=0, concat_axis=0, tiled=True)


FSDP_STEPS = (0, 1, 3, 2)


def ring(v, k):
    return lax.ppermute(v, "fsdp", [(i, (i + k) % 4) for i in range(4)]) if k % 4 else v


def fsdp_gather(v):
    return [ring(v, k) for k in FSDP_STEPS]


def fsdp_place(parts, f):
    out = jnp.zeros((4,) + parts[0].shape, parts[0].dtype)
    for k, v in zip(FSDP_STEPS, parts):
        out = lax.dynamic_update_index_in_dim(out, v, (f - k) % 4, 0)
    return out


def fsdp_exchange(v, f):
    return [ring(pick(v, (f + k) % 4), k) for k in FSDP_STEPS]


def total(parts):
    out = parts[0].astype(F32)
    for v in parts[1:]:
        out = out + v.astype(F32)
    return out


def swap_tp(v):
    return lax.ppermute(v, "tp", [(0, 1), (1, 0)])


def lanes(shape):
    return lax.broadcasted_iota(jnp.int32, shape, len(shape) - 1)


def half_swap(v, lane):
    return jnp.where(lane % HD < HD // 2, pltpu.roll(v, 96, 1), pltpu.roll(v, 32, 1))


def qkv_kernel(x_ref, w_ref, cos_ref, sin_ref, q_ref, kv_ref, n_ref, g_ref):
    x = x_ref[...]
    scale = lax.rsqrt(jnp.sum(x * x, axis=-1, keepdims=True) * (1.0 / DM) + EPS)
    pick = (
        lax.broadcasted_iota(jnp.int32, (8, 128), 0) + HD
        == lax.broadcasted_iota(jnp.int32, (8, 128), 1)
    ) & (lax.broadcasted_iota(jnp.int32, (8, 128), 0) < 2)
    gain_rows = dotd(jnp.where(pick, 1.0, 0.0).astype(BF), w_ref[:, 512:640], NT)
    g_ref[...] = gain_rows
    wide = lanes(x.shape)
    normed = jnp.where(wide % SLOT == ROWS, 1.0, x * scale * gain_rows[0:1]).astype(BF)
    n_ref[...] = normed
    proj = dot(normed, w_ref[:, 0:640])
    cosine = cos_ref[...]
    sine = sin_ref[...]
    lane = lanes(cosine.shape)
    left = lane < HD
    rots = []
    for g in range(4):
        v = proj[:, g * 128 : g * 128 + 128]
        rots.append(v * cosine + half_swap(v, lane) * sine)
    for h in range(7):
        r = rots[h // 2]
        if h % 2:
            r = pltpu.roll(r, HD, 1)
        qh = jnp.where(left, r * 0.125, 0.0).astype(BF)
        for s in range(2):
            for b in range(2):
                q_ref[s, b, h * 64 : h * 64 + 64, :] = qh[s * 128 + b * 64 : s * 128 + b * 64 + 64]
    pair = jnp.where(
        left, pltpu.roll(rots[3], HD, 1), pltpu.roll(proj[:, 512:640], HD, 1)
    ).astype(BF)
    for c in range(kv_ref.shape[0]):
        kv_ref[c] = pair


def order_rows(bo_ref, s, kv_ref, kvs):
    for j in range(32):
        at = pl.multiple_of(bo_ref[s, j] * 64, 64)
        kvs[pl.ds(at, 64), :] = kv_ref[j // 2, 0, (j % 2) * 64 : (j % 2) * 64 + 64, :]


def allowed(block, j):
    key = j * CH + lax.broadcasted_iota(jnp.int32, (448, CH), 1)
    query = block * 64 + lax.broadcasted_iota(jnp.int32, (448, CH), 0) % 64
    return key <= query


def attn_fwd_kernel(bo_ref, own_ref, q_ref, kv_ref, att_ref, lse_ref, kvs, sbuf, mbuf, lbuf, obuf):
    s = pl.program_id(0)
    order_rows(bo_ref, s, kv_ref, kvs)
    for b in range(2):
        block = own_ref[s, b]
        count = block // 4 + 1
        q = q_ref[0, b]
        mbuf[...] = jnp.full(mbuf.shape, MASKED, F32)

        def first(j, carry):
            k = kvs[pl.ds(pl.multiple_of(j * CH, CH), CH), :]
            sc = jnp.where(allowed(block, j), dotd(q, k, NT), MASKED)
            sbuf[j] = sc
            mbuf[...] = jnp.maximum(mbuf[...], jnp.maximum(sc[:, :128], sc[:, 128:]))
            return carry

        lax.fori_loop(0, count, first, 0)
        top = jnp.max(mbuf[...], axis=-1, keepdims=True)
        lbuf[...] = jnp.zeros(lbuf.shape, F32)
        obuf[...] = jnp.zeros(obuf.shape, F32)

        def second(j, carry):
            k = kvs[pl.ds(pl.multiple_of(j * CH, CH), CH), :]
            p = jnp.exp(sbuf[j] - top)
            lbuf[...] += p[:, :128] + p[:, 128:]
            obuf[...] += dot(p.astype(BF), k)
            return carry

        lax.fori_loop(0, count, second, 0)
        total = jnp.sum(lbuf[...], axis=-1, keepdims=True)
        lse_ref[0, b] = jnp.broadcast_to(top + jnp.log(total), (448, 128))
        o = obuf[...] / total
        left = lanes((64, 128)) < HD
        for g in range(4):
            even = pltpu.roll(o[g * 128 : g * 128 + 64], HD, 1)
            odd = o[g * 128 + 64 : g * 128 + 128] if g < 3 else jnp.zeros((64, 128), F32)
            att_ref[0, b * 64 : b * 64 + 64, g * 128 : g * 128 + 128] = jnp.where(
                left, even, odd
            ).astype(BF)


def head_rows(ref, b):
    right = lanes((64, 128)) >= HD
    parts = []
    for h in range(7):
        g = h // 2
        v = ref[0, b * 64 : b * 64 + 64, g * 128 : g * 128 + 128].astype(F32)
        if h % 2 == 0:
            v = pltpu.roll(v, HD, 1)
        parts.append(jnp.where(right, v, 0.0))
    return jnp.concatenate(parts, axis=0)


def attn_bwd_kernel(
    bo_ref, own_ref, q_ref, kv_ref, att_ref, do_ref, lse_ref, dq_ref, dkv_ref, kvs, dkvs, dqb
):
    s = pl.program_id(0)
    order_rows(bo_ref, s, kv_ref, kvs)
    dkvs[...] = jnp.zeros(dkvs.shape, F32)
    for b in range(2):
        block = own_ref[s, b]
        count = block // 4 + 1
        q = q_ref[0, b]
        do32 = head_rows(do_ref, b)
        delta = jnp.sum(do32 * head_rows(att_ref, b), axis=-1, keepdims=True)
        do = do32.astype(BF)
        lse = lse_ref[0, b][:, 0:1]
        dqb[...] = jnp.zeros(dqb.shape, F32)

        def step(j, carry):
            at = pl.ds(pl.multiple_of(j * CH, CH), CH)
            k = kvs[at, :]
            p = jnp.where(allowed(block, j), jnp.exp(dotd(q, k, NT) - lse), 0.0)
            ds = (p * (dotd(do, k, NT) - delta)).astype(BF)
            dqb[...] += dot(ds, k)
            dkvs[at, :] += dotd(ds, q, TN) + dotd(p.astype(BF), do, TN)
            return carry

        lax.fori_loop(0, count, step, 0)
        dq_ref[0, b] = dqb[...] * 0.125
    for j in range(32):
        at = pl.multiple_of(bo_ref[s, j] * 64, 64)
        dkv_ref[j // 2, 0, (j % 2) * 64 : (j % 2) * 64 + 64, :] = dkvs[pl.ds(at, 64), :].astype(BF)


def dproj_kernel(dq_ref, dkv_ref, cos_ref, sin_ref, w_ref, dp_ref, dn_ref):
    dkv = dkv_ref[0].astype(F32)
    for c in range(1, dkv_ref.shape[0]):
        dkv = dkv + dkv_ref[c].astype(F32)
    cosine = cos_ref[...]
    sine = sin_ref[...]
    lane = lanes(cosine.shape)
    left = lane < HD

    def head(h):
        return jnp.concatenate(
            [dq_ref[s, b, h * 64 : h * 64 + 64, :] for s in range(2) for b in range(2)], axis=0
        )

    for g in range(4):
        odd = head(2 * g + 1) if g < 3 else dkv
        u = jnp.where(left, head(2 * g), pltpu.roll(odd, HD, 1))
        dp_ref[:, g * 128 : g * 128 + 128] = (u * cosine - half_swap(u, lane) * sine).astype(BF)
    dp_ref[:, 512:640] = jnp.where(left, pltpu.roll(dkv, HD, 1), 0.0).astype(BF)
    dn_ref[...] = dotd(dp_ref[...], w_ref[:, 0:640], NT)


def mlp_kernel(n_ref, dm_ref, w_ref, act_ref, dg_ref, du_ref, dn_ref, out_ref):
    n = n_ref[...]
    gate = dot(n, w_ref[:, 0:FFB])
    up = dot(n, w_ref[:, FFB : 2 * FFB])
    dact = dot(dm_ref[...], w_ref[:, 2 * FFB : 3 * FFB])
    sg = 1.0 / (1.0 + jnp.exp(-gate))
    silu = gate * sg
    act = (silu * up).astype(BF)
    dg = (dact * up * sg * (1.0 + gate * (1.0 - sg))).astype(BF)
    du = (dact * silu).astype(BF)
    act_ref[...] = act
    dg_ref[...] = dg
    du_ref[...] = du
    dn_ref[...] = (dotd(dg, w_ref[:, 0:FFB], NT) + dotd(du, w_ref[:, FFB : 2 * FFB], NT)).astype(BF)
    out_ref[...] = dotd(act, w_ref[:, 2 * FFB : 3 * FFB], NT).astype(BF)


def wgrad_kernel(
    n0, n1, m0, m1, a0, a1, g0, g1, u0, u1, out_ref
):
    out_ref[:, 0:FFB] = (dotd(n0[...], g0[...], TN) + dotd(n1[...], g1[...], TN)).astype(BF)
    out_ref[:, FFB : 2 * FFB] = (dotd(n0[...], u0[...], TN) + dotd(n1[...], u1[...], TN)).astype(BF)
    out_ref[:, 2 * FFB : 3 * FFB] = (
        dotd(m0[...], a0[...], TN) + dotd(m1[...], a1[...], TN)
    ).astype(BF)


def call(kernel, outs, *args, name=None):
    return pl.pallas_call(
        kernel,
        out_shape=[jax.ShapeDtypeStruct(s, t) for s, t in outs],
        in_specs=[VMEM_ALL] * len(args),
        out_specs=[VMEM_ALL] * len(outs),
        compiler_params=PARAMS,
        name=name,
    )(*args)


def attn_fwd(bo, own, q, kv):
    return pl.pallas_call(
        attn_fwd_kernel,
        out_shape=[
            jax.ShapeDtypeStruct((2, 128, 512), BF),
            jax.ShapeDtypeStruct((2, 2, 448, 128), F32),
        ],
        grid_spec=pltpu.PrefetchScalarGridSpec(
            num_scalar_prefetch=2,
            grid=(2,),
            in_specs=[
                pl.BlockSpec((1, 2, 448, 128), lambda s, *_: (s, 0, 0, 0)),
                pl.BlockSpec((16, 1, 128, 128), lambda s, *_: (0, s, 0, 0)),
            ],
            out_specs=[
                pl.BlockSpec((1, 128, 512), lambda s, *_: (s, 0, 0)),
                pl.BlockSpec((1, 2, 448, 128), lambda s, *_: (s, 0, 0, 0)),
            ],
            scratch_shapes=[
                pltpu.VMEM((2048, 128), BF),
                pltpu.VMEM((8, 448, CH), F32),
                pltpu.VMEM((448, 128), F32),
                pltpu.VMEM((448, 128), F32),
                pltpu.VMEM((448, 128), F32),
            ],
        ),
        compiler_params=PARAMS,
        name="attn_fwd",
    )(bo, own, q, kv)


def attn_bwd(bo, own, q, kv, att, datt, lse):
    per_seq = pl.BlockSpec((1, 2, 448, 128), lambda s, *_: (s, 0, 0, 0))
    tokens = pl.BlockSpec((1, 128, 512), lambda s, *_: (s, 0, 0))
    pairs = pl.BlockSpec((16, 1, 128, 128), lambda s, *_: (0, s, 0, 0))
    return pl.pallas_call(
        attn_bwd_kernel,
        out_shape=[
            jax.ShapeDtypeStruct((2, 2, 448, 128), F32),
            jax.ShapeDtypeStruct((16, 2, 128, 128), BF),
        ],
        grid_spec=pltpu.PrefetchScalarGridSpec(
            num_scalar_prefetch=2,
            grid=(2,),
            in_specs=[per_seq, pairs, tokens, tokens, per_seq],
            out_specs=[per_seq, pairs],
            scratch_shapes=[
                pltpu.VMEM((2048, 128), BF),
                pltpu.VMEM((2048, 128), F32),
                pltpu.VMEM((448, 128), F32),
            ],
        ),
        compiler_params=PARAMS,
        name="attn_bwd",
    )(bo, own, q, kv, att, datt, lse)


def mlp(n, dm, w2):
    tok = pl.BlockSpec((256, DP), lambda i: (i, 0))
    hid = pl.BlockSpec((256, FFB), lambda i: (i, 0))
    return pl.pallas_call(
        mlp_kernel,
        out_shape=[jax.ShapeDtypeStruct((512, FFB), BF)] * 3
        + [jax.ShapeDtypeStruct((512, DP), BF)] * 2,
        grid=(2,),
        in_specs=[
            tok,
            tok,
            pl.BlockSpec((DP, 3 * FFB), lambda i: (0, 0), pipeline_mode=pl.Buffered(1)),
        ],
        out_specs=[hid, hid, hid, tok, tok],
        compiler_params=PARAMS,
        name="mlp",
    )(n, dm, w2)


def wgrads(n0, n1, m0, m1, first, second):
    feat = pl.BlockSpec((512, 256), lambda i: (0, i))
    hid = pl.BlockSpec((512, FFB), lambda i: (0, 0))
    args = [n0, n1, m0, m1, first[0], second[0], first[1], second[1], first[2], second[2]]
    return pl.pallas_call(
        wgrad_kernel,
        out_shape=jax.ShapeDtypeStruct((DP, 3 * FFB), BF),
        grid=(4,),
        in_specs=[feat] * 4 + [hid] * 6,
        out_specs=pl.BlockSpec((256, 3 * FFB), lambda i: (i, 0)),
        compiler_params=PARAMS,
        name="wgrad",
    )(*args)


def rms(v):
    scale = lax.rsqrt(jnp.sum(v * v, axis=-1, keepdims=True) * (1.0 / DM) + EPS)
    return v * scale, scale


def rms_back(dn, unit, scale, gain):
    e = dn * gain
    mean = jnp.sum(e * unit, axis=-1, keepdims=True) * (1.0 / DM)
    return scale * (e - unit * mean), jnp.sum(dn * unit, axis=0)


def pick(v, index):
    return lax.dynamic_index_in_dim(v, index, 0, keepdims=False)


def both(own, other, t):
    return jnp.stack([jnp.where(t == 0, own, other), jnp.where(t == 0, other, own)])


def tp_sum(own, other):
    return (own.astype(F32) + swap_tp(other).astype(F32)).astype(BF).reshape(4, 128, DP)


def fsdp_scatter(pair):
    return total([ring(pair[i], -k) for i, k in enumerate(FSDP_STEPS)])


def body(inputs, block_order, cotangent, gains, w_qkv, b_qkv, w_out, w_gate_up, w_down):
    seqs, toks, width = inputs.shape
    ctx = lax.axis_index("ctx")
    t = lax.axis_index("tp")
    f = lax.axis_index("fsdp")
    owner = f * 16 + ctx
    sel = selection()

    bias_row = jnp.where(jnp.arange(HD) == owner, b_qkv[0, 0], jnp.zeros((), BF)).reshape(1, 9 * HD)
    patch1 = jnp.concatenate(
        [
            jnp.concatenate([w_qkv[0, :, 0, :], bias_row, jnp.zeros((1, 9 * HD), BF)], axis=0),
            jnp.pad(gains[0].T, ((0, 2), (0, HD - 2))),
            jnp.pad(w_out[0, 0].T, ((0, 2), (0, 64))),
        ],
        axis=1,
    )
    w1 = spread(patch1, OWNERS, GRP).reshape(DP, 1152)
    wo = w1[:, 640:]

    tall = jnp.pad(w_gate_up[0], ((0, 2), (0, 0), (0, 4 * FFB - 2432)))
    gate_parts = tall[:, 0].reshape(SLOT, 4, FFB).transpose(1, 0, 2)
    up_parts = tall[:, 1].reshape(SLOT, 4, FFB).transpose(1, 0, 2)
    down_parts = (
        jnp.pad(w_down[0].T, ((0, 2), (0, 4 * FFB - 2432)))
        .reshape(SLOT, 4, FFB)
        .transpose(1, 0, 2)
    )
    patch2 = jnp.concatenate([gate_parts, up_parts, down_parts], axis=2)
    w2_own = fsdp_place(fsdp_exchange(patch2, f), f).reshape(64, 3 * FFB)
    w2 = lax.all_gather(w2_own, "ctx", axis=0, tiled=True)

    own = lax.dynamic_slice_in_dim(block_order, 2 * ctx, 2, 1)
    pos = (own[:, :, None] * 64 + jnp.arange(64, dtype=jnp.int32)).reshape(seqs * toks, 1)
    lane = lax.broadcasted_iota(jnp.int32, (1, 128), 1)
    freq = jnp.exp((lane % 32).astype(F32) * (-2.0 * math.log(ROPE_BASE) / HD))
    angle = pos.astype(F32) * freq
    cosine = jnp.cos(angle)
    sine = jnp.where(lane % HD < HD // 2, -1.0, 1.0) * jnp.sin(angle)

    x = pad_features(inputs.reshape(seqs * toks, width), sel)
    g = pad_features(cotangent.reshape(seqs * toks, width), sel)
    xh = pick(x.reshape(2, 128, DP), t)
    gh = pick(g.reshape(2, 128, DP), t)

    q, pairs, normed1, gain_rows = call(
        qkv_kernel,
        [((2, 2, 448, 128), BF), ((16, 256, 128), BF), ((256, DP), BF), ((8, DP), F32)],
        x, w1, cosine, sine, name="qkv",
    )
    gain1 = gain_rows[0:1]
    gain2 = gain_rows[1:2]
    kv = lax.all_to_all(pairs, "ctx", split_axis=0, concat_axis=0, tiled=True).reshape(
        16, 2, 128, 128
    )
    dm, _ = lax.optimization_barrier((gh.astype(BF), kv))
    m0 = jnp.concatenate(fsdp_gather(dm), axis=0)
    m1 = swap_tp(m0)
    att, lse = attn_fwd(block_order, own, q, kv)
    att, m0 = lax.optimization_barrier((att, m0))
    att2 = att.reshape(256, 512)
    mixed = dotd(att2, wo, NT).reshape(2, 128, DP)
    h2 = xh + (pick(mixed, t) + swap_tp(pick(mixed, 1 - t).astype(BF)).astype(F32))
    unit2, scale2 = rms(h2)
    n0 = jnp.concatenate(fsdp_gather((unit2 * gain2).astype(BF)), axis=0)
    n1 = swap_tp(n0)
    first = mlp(n0, m0, w2)
    second = mlp(n1, m1, w2)

    dn2 = fsdp_scatter(tp_sum(first[3], second[3]))
    out_pair = tp_sum(first[4], second[4])
    big = wgrads(n0, n1, m0, m1, first, second).reshape(OWNERS, SLOT, 3 * FFB)
    big, _ = lax.optimization_barrier((big, dn2))
    big = lax.all_to_all(big, GRP, split_axis=0, concat_axis=0, tiled=True)

    back2, gg2 = rms_back(dn2, unit2, scale2, gain2)
    g2 = gh + back2
    dah = g2.astype(BF)
    da = both(dah, swap_tp(dah), t).reshape(256, DP)
    datt = dot(da, wo).astype(BF).reshape(2, 128, 512)
    dq, dkv = attn_bwd(block_order, own, q, kv, att, datt, lse)
    dkv, big = lax.optimization_barrier((dkv, big))
    dkv = lax.all_to_all(dkv, "ctx", split_axis=0, concat_axis=0, tiled=True).reshape(16, 256, 128)
    out_pair, _ = lax.optimization_barrier((out_pair, dkv))
    dproj, dn1 = call(
        dproj_kernel, [((256, 640), BF), ((256, DP), F32)], dq, dkv, cosine, sine, w1, name="dproj"
    )
    dn1 = dn1.reshape(2, 128, DP)
    dn1h = pick(dn1, t) + swap_tp(pick(dn1, 1 - t).astype(BF)).astype(F32)
    unit1, scale1 = rms(xh)
    back1, gg1 = rms_back(dn1h, unit1, scale1, gain1)
    gin = unpad_features(g2 + back1, sel)
    grad_inputs = both(gin, swap_tp(gin), t)

    place = (jnp.arange(640)[None, :] == 576 + jnp.arange(2)[:, None]).astype(BF)
    gq = dotd(normed1, dproj, TN) + dotd(jnp.stack([gg1, gg2]).astype(BF), place, TN)
    last = jnp.concatenate([gq.astype(BF), dotd(da, att2, TN).astype(BF)], axis=1)
    last = lax.all_to_all(
        last.reshape(OWNERS, SLOT, 1152), GRP, split_axis=0, concat_axis=0, tiled=True
    )

    outh = h2 + fsdp_scatter(out_pair)
    outh = unpad_features(outh, sel)
    outputs = both(outh, swap_tp(outh), t)

    big = jnp.sum(big.reshape(16, 4, SLOT, 3 * FFB).astype(F32), axis=0)
    hidden = big[:, :ROWS, : 3 * FFB].transpose(1, 0, 2)

    def columns(k):
        return hidden[:, :, k * FFB : k * FFB + FFB].reshape(ROWS, 4 * FFB)[:, :2432]

    grad_gate_up = jnp.stack([columns(0), columns(1)], axis=1)[None]
    grad_down = columns(2).T[None]
    gq = jnp.sum(last.astype(F32), axis=0)
    grad_out = gq[:ROWS, 640:1088].T[None, None]
    grad_qkv = gq[None, :ROWS, None, :576]
    grad_bias = lax.dynamic_slice_in_dim(gq[ROWS, :576].reshape(9, HD), owner, 1, 1)[None, None]
    gg = gq[:ROWS, 576:578].T
    grad_gains = (gg + swap_tp(gg))[None]
    return (outputs, grad_inputs, grad_gains, grad_qkv, grad_bias, grad_out, grad_gate_up, grad_down)


def solution(mesh):
    in_specs = (
        P("fsdp", "ctx", None),
        P("fsdp", None),
        P("fsdp", "ctx", None),
        P(None, None, ("fsdp", "ctx")),
        P(None, ("fsdp", "ctx"), "tp", None),
        P(None, "tp", None, ("fsdp", "ctx")),
        P(None, "tp", None, ("fsdp", "ctx")),
        P(None, ("fsdp", "ctx"), None, "tp"),
        P(None, "tp", ("fsdp", "ctx")),
    )
    out_specs = (
        P("fsdp", "ctx", None),
        P("fsdp", "ctx", None),
        P(None, None, ("fsdp", "ctx")),
        P(None, ("fsdp", "ctx"), "tp", None),
        P(None, "tp", None, ("fsdp", "ctx")),
        P(None, "tp", None, ("fsdp", "ctx")),
        P(None, ("fsdp", "ctx"), None, "tp"),
        P(None, "tp", ("fsdp", "ctx")),
    )
    return jax.shard_map(body, mesh=mesh, in_specs=in_specs, out_specs=out_specs, check_vma=False)
```
